256 devices in a mesh: row: 16 (over y, z_hi, core), col: 16 (over z_lo, x).
Axes of the slice: x: 4, y: 4, z: 8 (z_hi: 2, z_lo: 4; z = z_hi * 4 + z_lo), core: 2. Of those that a mesh axis runs over, the one named last changes fastest.
Arguments:
- queries: bfloat16 [32, 16, 128, 2048], P('row', 'col'), may hold values from -70 to 70
- fine_keys: bfloat16 [32, 16, 128, 2048], P('row', 'col'), may hold values from -4 to 4
- fine_values: bfloat16 [32, 16, 128, 2048], P('row', 'col'), may hold values from -6 to 6
- keep_flags: int32 [32, 16, 9], P('row', 'col'), may hold values 0 or 1
- coarse_keys: bfloat16 [2048, 2048], P('col'), may hold values from -6 to 6
- coarse_values: bfloat16 [2048, 2048], P('col'), may hold values from -6 to 6
Outputs:
- attended: bfloat16 [32, 16, 128, 2048], P('row', 'col')
The draws below stay inside these ranges and needn't reach their ends.
All inputs are finite; a program needn't handle non-finite values. No bound on the sum of `keep_flags` on one device may be relied on, other than what follows from the above.
Results may differ from the reference program's by a relative error of at most 0.0035.
Values may be sent and summed in bfloat16 or wider, within the bound.
A program may use at most 128 MiB of HBM per device.

```python
import jax
import jax.numpy as jnp
from jax import lax

D = 2048
HEADS = 16
HEAD_DIM = 128
TILE = 128
NTR = 32
NTC = 16
COARSE = 2048


def drawn_pair(key):
    shape = (NTR, NTC, TILE, D)
    keys = jax.random.truncated_normal(jax.random.fold_in(key, 11), -4.0, 4.0, shape, jnp.float32)
    queries = 2.0 * jax.random.truncated_normal(jax.random.fold_in(key, 12), -4.0, 4.0, shape, jnp.float32)
    return (queries, keys)


def draw_queries(key, part):
    return drawn_pair(key)[0].astype(jnp.bfloat16)


def draw_fine_keys(key, part):
    return drawn_pair(key)[1].astype(jnp.bfloat16)


def plant(values, rng, low, top_value):
    longest = values.shape.index(max(values.shape))
    spots = []
    for shift in (0, 1):
        where = [jax.random.randint(jax.random.fold_in(rng, axis), (), 0, length) for axis, length in enumerate(values.shape)]
        where[longest] = (where[longest] + shift) % values.shape[longest]
        spots.append(tuple(where))
    return values.at[spots[0]].set(low).at[spots[1]].set(top_value)


def steps_of(key, dims, shards, low, top_value):
    def one(dim, blocks):
        draws = jax.random.uniform(jax.random.fold_in(jax.random.fold_in(key, 6), dim), (blocks,), jnp.float32, low / len(shards), top_value / len(shards))
        return jnp.repeat(jnp.exp(draws), dims[dim] // blocks).reshape((-1,) + (1,) * (len(dims) - dim - 1))

    factor_of = one(*shards[0])
    for cut in shards[1:]:
        factor_of = factor_of * one(*cut)
    return factor_of


def centred(key, shape, width, most, cuts=(), held_as=jnp.bfloat16):
    gain = steps_of(key, shape, cuts, -0.22, 0.18) if cuts else 1.0
    result = jax.random.normal(key, shape, jnp.float32) * width * gain
    return jnp.minimum(jnp.maximum(result, -most), most).astype(held_as)


def setup_inputs(seed: int = 0) -> dict:
    streams_of = jax.random.split(jax.random.key(seed), 7)
    queries = draw_queries(jax.random.fold_in(streams_of[6], 71), 0)
    fine_keys = draw_fine_keys(jax.random.fold_in(streams_of[6], 71), 0)
    fine_values = centred(streams_of[2], (NTR, NTC, TILE, D), 1.0, 6.0, ((0, 16), (1, 16)))
    keep_flags = plant((jax.random.randint(streams_of[3], (NTR, NTC, 9), 0, 3) < 2).astype(jnp.int32), jax.random.fold_in(streams_of[3], 1), 0, 1)
    coarse_keys = centred(streams_of[4], (COARSE, D), 1.0, 6.0, ((0, 16),))
    coarse_values = centred(streams_of[5], (COARSE, D), 1.0, 6.0, ((0, 16),))
    return dict(queries=queries, fine_keys=fine_keys, fine_values=fine_values, keep_flags=keep_flags, coarse_keys=coarse_keys, coarse_values=coarse_values)


def reference(queries, fine_keys, fine_values, keep_flags, coarse_keys, coarse_values):
    rows_total, cols_total, tile_len, model_width = queries.shape
    scale = HEAD_DIM ** -0.5
    stacked = jnp.stack((fine_keys, fine_values), 0)
    padded = jnp.pad(stacked, ((0, 0), (1, 1), (1, 1), (0, 0), (0, 0)))
    far_keys = coarse_keys.astype(jnp.float32).reshape(-1, HEADS, HEAD_DIM)
    far_values = coarse_values.astype(jnp.float32).reshape(-1, HEADS, HEAD_DIM)
    col_index = jnp.arange(cols_total)

    def one_row(row_at):
        band = lax.dynamic_slice_in_dim(padded, row_at, 3, 1)
        flag_row = lax.dynamic_index_in_dim(keep_flags, row_at, 0, False)
        pieces = []
        usable = []
        for row_step in range(3):
            for col_step in range(3):
                pieces.append(band[:, row_step, col_step:col_step + cols_total])
                grid_row = row_at + row_step - 1
                grid_col = col_index + col_step - 1
                inside = (grid_row >= 0) & (grid_row < rows_total) & (grid_col >= 0) & (grid_col < cols_total)
                kept_here = (flag_row[:, row_step * 3 + col_step] > 0) | (row_step == 1 and col_step == 1)
                usable.append(inside & kept_here)
        window = jnp.concatenate(pieces, axis=2).astype(jnp.float32)
        window_ok = jnp.repeat(jnp.stack(usable, 1), tile_len, axis=1)
        near_keys = window[0].reshape(cols_total, 9 * tile_len, HEADS, HEAD_DIM)
        near_values = window[1].reshape(cols_total, 9 * tile_len, HEADS, HEAD_DIM)
        query_row = lax.dynamic_index_in_dim(queries, row_at, 0, False).astype(jnp.float32)
        query_row = query_row.reshape(cols_total, tile_len, HEADS, HEAD_DIM)
        near_scores = jnp.einsum('tqhd,tkhd->thqk', query_row, near_keys) * scale
        near_scores = jnp.where(window_ok[:, None, None, :], near_scores, -jnp.inf)
        far_scores = jnp.einsum('tqhd,khd->thqk', query_row, far_keys) * scale
        largest = jnp.maximum(jnp.max(near_scores, -1), jnp.max(far_scores, -1))[..., None]
        near_probs = jnp.exp(near_scores - largest)
        far_probs = jnp.exp(far_scores - largest)
        total = jnp.sum(near_probs, -1) + jnp.sum(far_probs, -1)
        near_round = lax.optimization_barrier(near_probs.astype(jnp.bfloat16)).astype(jnp.float32)
        far_round = lax.optimization_barrier(far_probs.astype(jnp.bfloat16)).astype(jnp.float32)
        mixed = jnp.einsum('thqk,tkhd->tqhd', near_round, near_values)
        mixed = mixed + jnp.einsum('thqk,khd->tqhd', far_round, far_values)
        mixed = mixed / jnp.transpose(total, (0, 2, 1))[..., None]
        return mixed.reshape(cols_total, tile_len, model_width).astype(jnp.bfloat16)

    return lax.map(one_row, jnp.arange(rows_total))
```

```python
import jax
import jax.numpy as jnp
from jax import lax
from jax.experimental import pallas as pl
from jax.experimental.pallas import tpu as pltpu
from jax.sharding import PartitionSpec as P

HEAD_DIM = 128
NX, NY, NZ = 4, 4, 8
ZL = 4
PAIR = 256
LOG2E = 1.4426950408889634
MESH = pl.DeviceIdType.MESH

KE, VE, KI, VI, QQ, BB, CK, CV = 0, 8, 16, 24, 32, 40, 48, 52
CK2, CV2 = 56, 60
CK3, CV3 = 64, 80
RK, RV = 96, 104
HK, HV = 112, 114
XK, XV = 116, 120
OI, OE = 124, 132
SEMS = 140


def kernel(q_hbm, k_hbm, v_hbm, bias_hbm, ck_hbm, cv_hbm, out_hbm,
           qb, kb, vb, bb, ckb, cvb, ob, acc, mst, lst, ss, rs):
    row = lax.axis_index("row")
    col = lax.axis_index("col")
    core = lax.rem(row, 2)
    pair = row // 2
    zh = lax.rem(pair, 2)
    y = pair // 2
    x = lax.rem(col, NX)
    zl = col // NX
    z = zh * ZL + zl
    group = x * 2 + core

    def at(x_, y_, z_, c_):
        return ((y_ * 2 + z_ // ZL) * 2 + c_, lax.rem(z_, ZL) * NX + x_)

    def along_x(dx, dc):
        return at(lax.rem(x + dx, NX), y, z, lax.rem(core + dc, 2))

    def along_y(dy):
        return at(x, lax.rem(y + dy, NY), z, core)

    def along_z(dz):
        return at(x, y, lax.rem(z + dz + NZ, NZ), core)

    def along_p(dp):
        return (lax.rem(pair + dp + 8, 8) * 2 + core, col)

    mates = [(dx, dc) for dx in range(NX) for dc in range(2) if dx or dc]
    peers = [along_x(dx, dc) for dx, dc in mates]
    peers += [along_y(d) for d in (1, 2, 3)]
    peers += [along_z(d) for d in (1, -1, 2, -2)]
    peers += [along_p(d) for d in (1, -1)]
    barrier = pltpu.get_barrier_semaphore()
    for peer in peers:
        pl.semaphore_signal(barrier, inc=1, device_id=peer, device_id_type=MESH)

    sent = []
    kept = []

    def keep(src, dst, sem):
        copy = pltpu.make_async_copy(src, dst, rs.at[sem])
        copy.start()
        kept.append(copy)

    def send(src, dst, sem, peer):
        copy = pltpu.make_async_remote_copy(
            src_ref=src, dst_ref=dst, send_sem=ss.at[sem], recv_sem=rs.at[sem],
            device_id=peer, device_id_type=MESH)
        copy.start()
        sent.append(copy)

    def arrived(dst, sem):
        pltpu.make_async_copy(dst, dst, rs.at[sem]).wait()

    def lanes(g):
        return pl.ds(pl.multiple_of(g * PAIR, PAIR), PAIR)

    edge_row = 1 + 3 * core
    inner_row = 2 + core
    quarter = pl.ds(pl.multiple_of(y * 32, 32), 32)

    mine = lanes(group)
    keep(k_hbm.at[core, 0, :, mine], kb.at[edge_row, 1 + x], KE)
    keep(v_hbm.at[core, 0, :, mine], vb.at[edge_row, 1 + x], VE)
    keep(ck_hbm.at[quarter, mine], ckb.at[y, zl, x], CK)
    keep(cv_hbm.at[quarter, mine], cvb.at[y, zl, x], CV)
    keep(k_hbm.at[1 - core, 0, :, mine], kb.at[inner_row, 1 + x], KI)
    keep(v_hbm.at[1 - core, 0, :, mine], vb.at[inner_row, 1 + x], VI)
    keep(q_hbm.at[:, 0, :, mine], qb.at[pl.ds(2 * core, 2), x], QQ)
    keep(bias_hbm, bb.at[pl.ds(2 * core, 2), x], BB)

    pl.semaphore_wait(barrier, len(peers))

    for dx, dc in mates:
        cols = lanes(lax.rem(x + dx, NX) * 2 + lax.rem(core + dc, 2))
        send(k_hbm.at[core, 0, :, cols], kb.at[edge_row, 1 + x], KE + dx * 2 + dc, along_x(dx, dc))
        send(v_hbm.at[core, 0, :, cols], vb.at[edge_row, 1 + x], VE + dx * 2 + dc, along_x(dx, dc))
    for dx in (1, 2, 3):
        cols = lanes(lax.rem(x + dx, NX) * 2 + core)
        send(ck_hbm.at[quarter, cols], ckb.at[y, zl, x], CK + dx, along_x(dx, 0))
        send(cv_hbm.at[quarter, cols], cvb.at[y, zl, x], CV + dx, along_x(dx, 0))
    for dx, dc in mates:
        cols = lanes(lax.rem(x + dx, NX) * 2 + lax.rem(core + dc, 2))
        send(k_hbm.at[1 - core, 0, :, cols], kb.at[inner_row, 1 + x], KI + dx * 2 + dc, along_x(dx, dc))
        send(v_hbm.at[1 - core, 0, :, cols], vb.at[inner_row, 1 + x], VI + dx * 2 + dc, along_x(dx, dc))
    for dx, dc in mates:
        cols = lanes(lax.rem(x + dx, NX) * 2 + lax.rem(core + dc, 2))
        send(q_hbm.at[:, 0, :, cols], qb.at[pl.ds(2 * core, 2), x], QQ + dx * 2 + dc, along_x(dx, dc))
        send(bias_hbm, bb.at[pl.ds(2 * core, 2), x], BB + dx * 2 + dc, along_x(dx, dc))

    for j in (0, 3, 1, 2):
        dx = lax.rem(x + NX - j, NX)
        for top in (0, 1):
            dc = lax.rem(core + top, 2)
            src_row, dst_row, peer = ((1, 5, along_p(-1)), (4, 0, along_p(1)))[top]
            arrived(kb.at[src_row, 1 + j], KE + dx * 2 + dc)
            send(kb.at[src_row, 1 + j], kb.at[dst_row, 1 + j], RK + top * 4 + j, peer)
            arrived(vb.at[src_row, 1 + j], VE + dx * 2 + dc)
            send(vb.at[src_row, 1 + j], vb.at[dst_row, 1 + j], RV + top * 4 + j, peer)

    for buf, first, second, far in ((ckb, CK, CK2, 2), (cvb, CV, CV2, -2)):
        for dx in range(NX):
            arrived(buf.at[y, zl, lax.rem(x + NX - dx, NX)], first + dx)
        send(buf.at[y, zl], buf.at[y, zl], second + 1, along_z(1))
        send(buf.at[y, zl], buf.at[y, zl], second + 3, along_z(-1))
        send(buf.at[y, zl], buf.at[y, zl], second + 2, along_z(far))

    for dx in range(NX):
        j = lax.rem(x + NX - dx, NX)
        for s in (0, 1):
            dc = lax.rem(core + s, 2)
            arrived(kb.at[2 + s, 1 + j], KI + dx * 2 + dc)
            arrived(vb.at[2 + s, 1 + j], VI + dx * 2 + dc)
    for buf, sem in ((kb, HK), (vb, HV)):
        send(buf.at[pl.ds(1, 4), 4], buf.at[pl.ds(1, 4), 0], sem, along_z(1))
        send(buf.at[pl.ds(1, 4), 1], buf.at[pl.ds(1, 4), 5], sem + 1, along_z(-1))

    for dz in (0, 1, 3, 2):
        from_zl = lax.rem(zl + ZL - dz, ZL)
        for buf, second, third in ((ckb, CK2, CK3), (cvb, CV2, CV3)):
            if dz:
                arrived(buf.at[y, from_zl], second + dz)
            for dy in (1, 2, 3):
                send(buf.at[y, from_zl], buf.at[y, from_zl], third + dz * 4 + dy, along_y(dy))

    for dx in range(NX):
        j = lax.rem(x + NX - dx, NX)
        for dc in (0, 1):
            half = pl.ds(2 * lax.rem(core + dc, 2), 2)
            arrived(qb.at[half, j], QQ + dx * 2 + dc)
            arrived(bb.at[half, j], BB + dx * 2 + dc)
    for buf, sem in ((kb, HK), (vb, HV)):
        arrived(buf.at[pl.ds(1, 4), 0], sem)
        arrived(buf.at[pl.ds(1, 4), 5], sem + 1)
    for dz in range(ZL):
        from_zl = lax.rem(zl + ZL - dz, ZL)
        for buf, third in ((ckb, CK3), (cvb, CV3)):
            for dy in (1, 2, 3):
                arrived(buf.at[lax.rem(y + NY - dy, NY), from_zl], third + dz * 4 + dy)

    factor = LOG2E * HEAD_DIM ** -0.5
    contract = (((1,), (1,)), ((), ()))

    def near(i, j, h, a):
        heads = slice(h * HEAD_DIM, (h + 1) * HEAD_DIM)
        keys = kb[i + a, pl.ds(j, 3), :, heads].reshape(3 * 128, HEAD_DIM)
        values = vb[i + a, pl.ds(j, 3), :, heads].reshape(3 * 128, HEAD_DIM)
        return keys, values, bb[i, j, a:a + 1, :]

    def attend(i, j, h, rows, coarse):
        heads = slice(h * HEAD_DIM, (h + 1) * HEAD_DIM)
        query = qb[i, j, :, heads]
        scores, values = [], []
        for a in rows:
            keys, vals, bias = near(i, j, h, a)
            scores.append(lax.dot_general(query, keys, contract, preferred_element_type=jnp.float32) + bias)
            values.append(vals)
        if coarse:
            keys = ckb[:, :, :, :, heads].reshape(2048, HEAD_DIM)
            scores.append(lax.dot_general(query, keys, contract, preferred_element_type=jnp.float32))
            values.append(cvb[:, :, :, :, heads].reshape(2048, HEAD_DIM))
        return scores, values

    def combine(scores, values, floor):
        largest = scores[0].max(-1, keepdims=True)
        for s in scores[1:]:
            largest = jnp.maximum(largest, s.max(-1, keepdims=True))
        if floor is not None:
            largest = jnp.maximum(largest, floor)
        total, mixed = None, None
        shift = largest * factor
        for s, v in zip(scores, values):
            p = jnp.exp2(s * factor - shift)
            t = p.sum(-1, keepdims=True)
            o = jnp.dot(p.astype(jnp.bfloat16), v, preferred_element_type=jnp.float32)
            total = t if total is None else total + t
            mixed = o if mixed is None else mixed + o
        return largest, total, mixed

    def give_back(out_sem, source_row, tile_of):
        for dx in range(NX):
            for dc in (0, 1):
                to_x = lax.rem(x + dx, NX)
                to_c = lax.rem(core + dc, 2)
                src = ob.at[source_row(to_c), to_x]
                dst = out_hbm.at[tile_of(to_c), 0, :, mine]
                if dx or dc:
                    send(src, dst, out_sem + dx * 2 + dc, along_x(dx, dc))
                else:
                    keep(src, dst, out_sem)

    def get_back(out_sem, tile):
        for dx in range(NX):
            for dc in (0, 1):
                g = lax.rem(x + NX - dx, NX) * 2 + lax.rem(core + dc, 2)
                arrived(out_hbm.at[tile, 0, :, lanes(g)], out_sem + dx * 2 + dc)

    @pl.loop(0, 8)
    def _(t):
        i, j = 1 + t // 4, lax.rem(t, 4)
        for h in (0, 1):
            scores, values = attend(i, j, h, (0, 1, 2), True)
            _, total, mixed = combine(scores, values, None)
            ob[i, j, :, h * HEAD_DIM:(h + 1) * HEAD_DIM] = (mixed / total).astype(jnp.bfloat16)

    give_back(OI, lambda c: 1 + c, lambda c: 1 - c)

    for j, src_col, dst_col, dz, which in ((3, 4, 0, 1, 0), (0, 1, 5, -1, 1)):
        for top, r in ((0, 5), (1, 0)):
            for buf, rsem, xsem in ((kb, RK, XK), (vb, RV, XV)):
                arrived(buf.at[r, src_col], rsem + top * 4 + j)
                send(buf.at[r, src_col], buf.at[r, dst_col], xsem + which * 2 + top, along_z(dz))

    for i, rows in ((0, (1, 2)), (3, (0, 1))):
        @pl.loop(0, 4)
        def _(j):
            for h in (0, 1):
                scores, values = attend(i, j, h, rows, True)
                largest, total, mixed = combine(scores, values, None)
                at_ = (i // 3) * 4 + j
                acc[h, at_] = mixed
                mst[h, at_] = jnp.broadcast_to(largest, (128, 128))
                lst[h, at_] = jnp.broadcast_to(total, (128, 128))

    for top, r in ((0, 5), (1, 0)):
        for buf, rsem, xsem in ((kb, RK, XK), (vb, RV, XV)):
            for j in (1, 2):
                arrived(buf.at[r, 1 + j], rsem + top * 4 + j)
            arrived(buf.at[r, 0], xsem + top)
            arrived(buf.at[r, 5], xsem + 2 + top)

    for i, a in ((0, 0), (3, 2)):
        @pl.loop(0, 4)
        def _(j):
            for h in (0, 1):
                at_ = (i // 3) * 4 + j
                scores, values = attend(i, j, h, (a,), False)
                before = mst[h, at_]
                largest, total, mixed = combine(scores, values, before[:, :1])
                scale = jnp.exp2((before - largest) * factor)
                mixed = mixed + acc[h, at_] * scale
                total = total + lst[h, at_] * scale
                ob[i, j, :, h * HEAD_DIM:(h + 1) * HEAD_DIM] = (mixed / total).astype(jnp.bfloat16)

    give_back(OE, lambda c: 3 * c, lambda c: c)
    get_back(OI, 1 - core)
    get_back(OE, core)
    for copy in sent:
        copy.wait_send()


def body(queries, fine_keys, fine_values, keep_flags, coarse_keys, coarse_values):
    rows_tiles = queries.shape[0]
    steps = jnp.arange(3) - 1
    grid_row = lax.axis_index("row") * rows_tiles + jnp.arange(rows_tiles)[:, None, None] + steps[None, :, None]
    grid_col = lax.axis_index("col") + steps[None, None, :]
    inside = (grid_row >= 0) & (grid_row < rows_tiles * lax.axis_size("row"))
    inside = inside & (grid_col >= 0) & (grid_col < lax.axis_size("col"))
    own = (steps[:, None] == 0) & (steps[None, :] == 0)
    usable = inside & ((keep_flags.reshape(rows_tiles, 3, 3) > 0) | own[None])
    bias = jnp.where(usable, 0.0, -jnp.inf).astype(jnp.float32)
    bias = jnp.broadcast_to(bias[..., None], (rows_tiles, 3, 3, 128)).reshape(rows_tiles, 3, 384)
    bias = jnp.pad(bias, ((0, 0), (0, 5), (0, 0)))
    bf16, f32 = jnp.bfloat16, jnp.float32
    return pl.pallas_call(
        kernel,
        out_shape=jax.ShapeDtypeStruct(queries.shape, bf16),
        in_specs=[pl.BlockSpec(memory_space=pl.ANY)] * 6,
        out_specs=pl.BlockSpec(memory_space=pl.ANY),
        scratch_shapes=[
            pltpu.VMEM((4, 4, 128, PAIR), bf16),
            pltpu.VMEM((6, 6, 128, PAIR), bf16),
            pltpu.VMEM((6, 6, 128, PAIR), bf16),
            pltpu.VMEM((4, 4, 8, 384), f32),
            pltpu.VMEM((NY, ZL, NX, 32, PAIR), bf16),
            pltpu.VMEM((NY, ZL, NX, 32, PAIR), bf16),
            pltpu.VMEM((4, 4, 128, PAIR), bf16),
            pltpu.VMEM((2, 8, 128, 128), f32),
            pltpu.VMEM((2, 8, 128, 128), f32),
            pltpu.VMEM((2, 8, 128, 128), f32),
            pltpu.SemaphoreType.DMA((SEMS,)),
            pltpu.SemaphoreType.DMA((SEMS,)),
        ],
        compiler_params=pltpu.CompilerParams(
            collective_id=0, has_side_effects=True, vmem_limit_bytes=48 << 20),
        name="window_attention",
    )(queries, fine_keys, fine_values, bias, coarse_keys, coarse_values)


def solution(mesh):
    placed = (
        P("row", "col", None, None),
        P("row", "col", None, None),
        P("row", "col", None, None),
        P("row", "col", None),
        P("col", None),
        P("col", None),
    )
    return jax.shard_map(
        body, mesh=mesh, in_specs=placed, out_specs=P("row", "col", None, None), check_vma=False
    )
```

```python
import jax
import jax.numpy as jnp
from jax import lax
from jax.experimental import pallas as pl
from jax.experimental.pallas import tpu as pltpu
from jax.sharding import PartitionSpec as P

HEAD_DIM = 128
NX, NY, NZ = 4, 4, 8
ZL = 4
NP = 8
PAIR = 256
LOG2E = 1.4426950408889634
MESH = pl.DeviceIdType.MESH

KE, VE, KI, VI, QQ, BB = 0, 8, 16, 24, 32, 40
CZK, CZV = 48, 52
CXK, CXV = 56, 60
CYK, CYV = 64, 68
RK, RV = 72, 84
HK, HV = 96, 98
OI, OE = 100, 108
FLAGS = 116
SEMS = 117


def kernel(q_hbm, k_hbm, v_hbm, flags_hbm, ck_hbm, cv_hbm, out_hbm,
           qb, kb, vb, flags, bias, bb, zk, zv, ckb, cvb, ob, acc, mst, lst, ss, rs):
    row = lax.axis_index("row")
    col = lax.axis_index("col")
    core = lax.rem(row, 2)
    pair = row // 2
    zh = lax.rem(pair, 2)
    y = pair // 2
    x = lax.rem(col, NX)
    zl = col // NX
    z = zh * ZL + zl

    def at(x_, y_, z_, c_):
        return ((y_ * 2 + z_ // ZL) * 2 + c_, lax.rem(z_, ZL) * NX + x_)

    def along_x(dx, dc):
        return at(lax.rem(x + dx, NX), y, z, lax.rem(core + dc, 2))

    def along_y(dy):
        return at(x, lax.rem(y + dy, NY), z, core)

    def along_z(dz):
        return at(x, y, lax.rem(z + dz + NZ, NZ), core)

    def halo_target(dp, dz):
        band = lax.rem(pair + dp + NP, NP)
        z_ = lax.rem(lax.rem(band, 2) * ZL + zl + dz + NZ, NZ)
        return at(x, band // 2, z_, core)

    def halo_source(dp, dz):
        z_ = lax.rem(z - dz + NZ, NZ)
        band = lax.rem(y * 2 + z_ // ZL - dp + NP, NP)
        return (band * 2 + core, lax.rem(z_, ZL) * NX + x)

    mates = [(dx, dc) for dx in (0, 1, 3, 2) for dc in (1, 0) if dx or dc]
    callers = [along_x(dx, dc) for dx, dc in mates]
    callers += [along_y(d) for d in (1, 2, 3)]
    callers += [along_z(d) for d in (1, -1, 2, -2)]
    callers += [halo_source(dp, dz) for dp in (1, -1) for dz in (-1, 0, 1)]
    barrier = pltpu.get_barrier_semaphore()
    for peer in callers:
        pl.semaphore_signal(barrier, inc=1, device_id=peer, device_id_type=MESH)

    sent = []

    def keep(src, dst, sem):
        pltpu.make_async_copy(src, dst, rs.at[sem]).start()

    def send(src, dst, sem, peer):
        copy = pltpu.make_async_remote_copy(
            src_ref=src, dst_ref=dst, send_sem=ss.at[sem], recv_sem=rs.at[sem],
            device_id=peer, device_id_type=MESH)
        copy.start()
        sent.append(copy)

    def arrived(dst, sem):
        pltpu.make_async_copy(dst, dst, rs.at[sem]).wait()

    def lanes(g):
        return pl.ds(pl.multiple_of(g * PAIR, PAIR), PAIR)

    def heads_of(dx, dc):
        return lanes(lax.rem(core + dc, 2) * NX + lax.rem(x + dx, NX))

    def x_back(dx):
        return lax.rem(x + NX - dx, NX)

    edge_row = 1 + 3 * core
    inner_row = 2 + core
    both_rows = pl.ds(2 * core, 2)
    quarter = pl.ds(pl.multiple_of(y * 32, 32), 32)
    half = pl.ds(pl.multiple_of(core * 1024, 1024), 1024)
    mine = heads_of(0, 0)

    keep(flags_hbm, flags, FLAGS)
    keep(k_hbm.at[core, 0, :, mine], kb.at[edge_row, 1 + x], KE)
    keep(v_hbm.at[core, 0, :, mine], vb.at[edge_row, 1 + x], VE)
    keep(ck_hbm.at[quarter, half], zk.at[zl], CZK)
    keep(cv_hbm.at[quarter, half], zv.at[zl], CZV)
    keep(q_hbm.at[:, 0, :, mine], qb.at[both_rows, x], QQ)
    keep(k_hbm.at[1 - core, 0, :, mine], kb.at[inner_row, 1 + x], KI)
    keep(v_hbm.at[1 - core, 0, :, mine], vb.at[inner_row, 1 + x], VI)

    bias[...] = jnp.zeros(bias.shape, jnp.float32)
    arrived(flags, FLAGS)
    for t in range(2):
        kept = flags[t]
        for a in range(3):
            for b in range(3):
                cell = (slice(a, a + 1), slice(b * 128, (b + 1) * 128))
                if a == 1 and b == 1:
                    continue
                grid_row = row * 2 + t + a - 1
                grid_col = col + b - 1
                inside = ((grid_row >= 0) & (grid_row < 2 * 2 * NP)
                          & (grid_col >= 0) & (grid_col < ZL * NX))
                flag = jnp.broadcast_to(kept[:, 3 * a + b:3 * a + b + 1], (1, 128))
                usable = (flag > 0) & jnp.broadcast_to(inside, (1, 128))
                bias[(t, *cell)] = jnp.where(usable, 0.0, -jnp.inf).astype(jnp.float32)
    keep(bias, bb.at[both_rows, x], BB)

    pl.semaphore_wait(barrier, len(callers))

    for src, buf, sem, far in ((ck_hbm, zk, CZK, 2), (cv_hbm, zv, CZV, -2)):
        send(src.at[quarter, half], buf.at[zl], sem + 1, along_z(1))
        send(src.at[quarter, half], buf.at[zl], sem + 3, along_z(-1))
        send(src.at[quarter, half], buf.at[zl], sem + 2, along_z(far))
    for dx, dc in mates:
        for src, buf, sem in ((k_hbm, kb, KE), (v_hbm, vb, VE)):
            send(src.at[core, 0, :, heads_of(dx, dc)], buf.at[edge_row, 1 + x], sem + dx * 2 + dc, along_x(dx, dc))

    def forward_rows(dx):
        j = x_back(dx)
        first, last = (3 - j) // 3, j // 3
        dst_col = 1 + j + 4 * first - 4 * last
        slot = j + 4 * first + 2 * last
        for top in (0, 1):
            dc = lax.rem(core + top, 2)
            src_row, dst_row, dp = ((1, 5, -1), (4, 0, 1))[top]
            for buf, esem, sem in ((kb, KE, RK), (vb, VE, RV)):
                arrived(buf.at[src_row, 1 + j], esem + dx * 2 + dc)
                send(buf.at[src_row, 1 + j], buf.at[dst_row, dst_col], sem + top * 6 + slot,
                     halo_target(dp, last - first))

    forward_rows(0)
    for buf, sem in ((zk, CZK), (zv, CZV)):
        for dz in range(ZL):
            arrived(buf.at[lax.rem(zl + ZL - dz, ZL)], sem + dz)
    for zbuf, buf, sem in ((zk, ckb, CXK), (zv, cvb, CXV)):
        for dx in (1, 3, 2):
            send(zbuf.at[:, :, lanes(lax.rem(x + dx, NX))], buf.at[y, :, x], sem + dx, along_x(dx, 0))
        keep(zbuf.at[:, :, lanes(x)], buf.at[y, :, x], sem)
    forward_rows(1)
    forward_rows(3)
    for dx, dc in mates:
        send(q_hbm.at[:, 0, :, heads_of(dx, dc)], qb.at[both_rows, x], QQ + dx * 2 + dc, along_x(dx, dc))
    forward_rows(2)
    for dx, dc in mates:
        send(bias, bb.at[both_rows, x], BB + dx * 2 + dc, along_x(dx, dc))
        for src, buf, sem in ((k_hbm, kb, KI), (v_hbm, vb, VI)):
            send(src.at[1 - core, 0, :, heads_of(dx, dc)], buf.at[inner_row, 1 + x], sem + dx * 2 + dc, along_x(dx, dc))

    for buf, xsem, ysem in ((ckb, CXK, CYK), (cvb, CXV, CYV)):
        for dx in range(NX):
            arrived(buf.at[y, :, x_back(dx)], xsem + dx)
        for dy in (1, 3, 2):
            send(buf.at[y], buf.at[y], ysem + dy, along_y(dy))

    factor = LOG2E * HEAD_DIM ** -0.5
    contract = (((1,), (1,)), ((), ()))

    def scored(i, j, h, near, coarse):
        heads = slice(h * HEAD_DIM, (h + 1) * HEAD_DIM)
        query = qb[i, j, :, heads]
        scores, values = [], []
        for a in near:
            keys = kb[i + a, pl.ds(j, 3), :, heads].reshape(3 * 128, HEAD_DIM)
            s = lax.dot_general(query, keys, contract, preferred_element_type=jnp.float32)
            scores.append(s + bb[i, j, a:a + 1, :])
            values.append(vb[i + a, pl.ds(j, 3), :, heads].reshape(3 * 128, HEAD_DIM))
        for dy in coarse:
            q_at = lax.rem(y + NY - dy, NY)
            keys = ckb[q_at, :, :, :, heads].reshape(512, HEAD_DIM)
            scores.append(lax.dot_general(query, keys, contract, preferred_element_type=jnp.float32))
            values.append(cvb[q_at, :, :, :, heads].reshape(512, HEAD_DIM))
        return scores, values

    def unit(i, j, near, coarse, start, finish):
        for h in (0, 1):
            scores, values = scored(i, j, h, near, coarse)
            slot = i * 4 + j
            largest = scores[0].max(-1, keepdims=True)
            for s in scores[1:]:
                largest = jnp.maximum(largest, s.max(-1, keepdims=True))
            if not start:
                before = mst[h, slot]
                largest = jnp.maximum(largest, before[:, :1])
            shift = largest * factor
            total, mixed = None, None
            for s, v in zip(scores, values):
                p = jnp.exp2(s * factor - shift)
                t = p.sum(-1, keepdims=True)
                o = jnp.dot(p.astype(jnp.bfloat16), v, preferred_element_type=jnp.float32)
                total = t if total is None else total + t
                mixed = o if mixed is None else mixed + o
            if not start:
                scale = jnp.exp2((before - largest) * factor)
                mixed = mixed + acc[h, slot] * scale
                total = total + lst[h, slot] * scale
            if finish:
                ob[i, j, :, h * HEAD_DIM:(h + 1) * HEAD_DIM] = (mixed / total).astype(jnp.bfloat16)
            else:
                acc[h, slot] = mixed
                mst[h, slot] = jnp.broadcast_to(largest, (128, 128))
                lst[h, slot] = jnp.broadcast_to(total, (128, 128))

    def give_back(out_sem, source_row, tile_of):
        for dx in (1, 3, 2, 0):
            for dc in (1, 0):
                to_x = lax.rem(x + dx, NX)
                to_c = lax.rem(core + dc, 2)
                src = ob.at[source_row(to_c), to_x]
                dst = out_hbm.at[tile_of(to_c), 0, :, mine]
                if dx or dc:
                    send(src, dst, out_sem + dx * 2 + dc, along_x(dx, dc))
                else:
                    keep(src, dst, out_sem)

    def get_back(out_sem, tile):
        for dx in range(NX):
            for dc in (0, 1):
                g = lax.rem(core + dc, 2) * NX + x_back(dx)
                arrived(out_hbm.at[tile, 0, :, lanes(g)], out_sem + dx * 2 + dc)

    for dx in range(NX):
        for dc in (0, 1):
            rows = pl.ds(2 * lax.rem(core + dc, 2), 2)
            arrived(qb.at[rows, x_back(dx)], QQ + dx * 2 + dc)
    for buf, ysem in ((ckb, CYK), (cvb, CYV)):
        arrived(buf.at[lax.rem(y + NY - 1, NY)], ysem + 1)

    @pl.loop(0, 16)
    def _(t):
        unit(t // 4, lax.rem(t, 4), (), (0, 1), True, False)

    for dx in range(NX):
        j = x_back(dx)
        for s in (0, 1):
            dc = lax.rem(core + s, 2)
            arrived(kb.at[2 + s, 1 + j], KI + dx * 2 + dc)
            arrived(vb.at[2 + s, 1 + j], VI + dx * 2 + dc)
    for buf, sem in ((kb, HK), (vb, HV)):
        send(buf.at[pl.ds(1, 4), 4], buf.at[pl.ds(1, 4), 0], sem, along_z(1))
        send(buf.at[pl.ds(1, 4), 1], buf.at[pl.ds(1, 4), 5], sem + 1, along_z(-1))
    for top, r in ((0, 5), (1, 0)):
        for buf, sem in ((kb, RK), (vb, RV)):
            for slot, from_col, to_col, j, dz in ((4, 5, 1, 0, 1), (5, 0, 4, 3, -1)):
                arrived(buf.at[r, from_col], sem + top * 6 + slot)
                send(buf.at[r, from_col], buf.at[r, to_col], sem + top * 6 + j, along_z(dz))

    for buf, ysem in ((ckb, CYK), (cvb, CYV)):
        for dy in (3, 2):
            arrived(buf.at[lax.rem(y + NY - dy, NY)], ysem + dy)

    @pl.loop(0, 16)
    def _(t):
        unit(t // 4, lax.rem(t, 4), (), (2, 3), False, False)

    for dx in range(NX):
        for dc in (0, 1):
            rows = pl.ds(2 * lax.rem(core + dc, 2), 2)
            arrived(bb.at[rows, x_back(dx)], BB + dx * 2 + dc)
    for buf, sem in ((kb, HK), (vb, HV)):
        arrived(buf.at[pl.ds(1, 4), 0], sem)
        arrived(buf.at[pl.ds(1, 4), 5], sem + 1)

    @pl.loop(0, 8)
    def _(t):
        unit(1 + t // 4, lax.rem(t, 4), (0, 1, 2), (), False, True)

    give_back(OI, lambda c: 1 + c, lambda c: 1 - c)

    for i, rows in ((0, (1, 2)), (3, (0, 1))):
        @pl.loop(0, 4)
        def _(j):
            unit(i, j, rows, (), False, False)

    for top, r, i, a in ((0, 5, 3, 2), (1, 0, 0, 0)):
        for buf, sem in ((kb, RK), (vb, RV)):
            for j in range(4):
                arrived(buf.at[r, 1 + j], sem + top * 6 + j)

    for i, a in ((0, 0), (3, 2)):
        @pl.loop(0, 4)
        def _(j):
            unit(i, j, (a,), (), False, True)

    give_back(OE, lambda c: 3 * c, lambda c: c)
    get_back(OI, 1 - core)
    get_back(OE, core)
    for copy in sent:
        copy.wait_send()


def body(queries, fine_keys, fine_values, keep_flags, coarse_keys, coarse_values):
    bf16, f32 = jnp.bfloat16, jnp.float32
    return pl.pallas_call(
        kernel,
        out_shape=jax.ShapeDtypeStruct(queries.shape, bf16),
        in_specs=[pl.BlockSpec(memory_space=pltpu.HBM)] * 6,
        out_specs=pl.BlockSpec(memory_space=pltpu.HBM),
        scratch_shapes=[
            pltpu.VMEM((4, 4, 128, PAIR), bf16),
            pltpu.VMEM((6, 6, 128, PAIR), bf16),
            pltpu.VMEM((6, 6, 128, PAIR), bf16),
            pltpu.VMEM((2, 1, 9), jnp.int32),
            pltpu.VMEM((2, 8, 384), f32),
            pltpu.VMEM((4, 4, 8, 384), f32),
            pltpu.VMEM((ZL, 32, 1024), bf16),
            pltpu.VMEM((ZL, 32, 1024), bf16),
            pltpu.VMEM((NY, ZL, NX, 32, PAIR), bf16),
            pltpu.VMEM((NY, ZL, NX, 32, PAIR), bf16),
            pltpu.VMEM((4, 4, 128, PAIR), bf16),
            pltpu.VMEM((2, 16, 128, 128), f32),
            pltpu.VMEM((2, 16, 128, 128), f32),
            pltpu.VMEM((2, 16, 128, 128), f32),
            pltpu.SemaphoreType.DMA((SEMS,)),
            pltpu.SemaphoreType.DMA((SEMS,)),
        ],
        compiler_params=pltpu.CompilerParams(
            collective_id=0, has_side_effects=True, vmem_limit_bytes=VMEM_LIMIT),
        name="window_attention",
    )(queries, fine_keys, fine_values, keep_flags, coarse_keys, coarse_values)


VMEM_LIMIT = 63 << 20


def solution(mesh):
    placed = (
        P("row", "col", None, None),
        P("row", "col", None, None),
        P("row", "col", None, None),
        P("row", "col", None),
        P("col", None),
        P("col", None),
    )
    return jax.shard_map(
        body, mesh=mesh, in_specs=placed, out_specs=P("row", "col", None, None), check_vma=False
    )
```

```python
import jax
import jax.numpy as jnp
from jax import lax
from jax.experimental import pallas as pl
from jax.experimental.pallas import tpu as pltpu
from jax.sharding import PartitionSpec as P

HEAD_DIM = 128
NX, NY, NZ = 4, 4, 8
ZL = 4
NP = 8
PAIR = 256
LOG2E = 1.4426950408889634
MESH = pl.DeviceIdType.MESH

KE, VE, KI, VI, QQ, BB = 0, 8, 16, 24, 32, 40
CZK, CZV = 48, 52
CXK, CXV = 56, 60
CYK, CYV = 64, 68
RK, RV = 72, 84
HK, HV = 96, 98
OI, OE = 100, 108
FLAGS = 116
SEMS = 117


def kernel(q_hbm, k_hbm, v_hbm, flags_hbm, ck_hbm, cv_hbm, out_hbm,
           qb, kb, vb, flags, bias, bb, zk, zv, ckb, cvb, ob, acc, mst, lst, ss, rs):
    row = lax.axis_index("row")
    col = lax.axis_index("col")
    core = lax.rem(row, 2)
    pair = row // 2
    zh = lax.rem(pair, 2)
    y = pair // 2
    x = lax.rem(col, NX)
    zl = col // NX
    z = zh * ZL + zl

    def at(x_, y_, z_, c_):
        return ((y_ * 2 + z_ // ZL) * 2 + c_, lax.rem(z_, ZL) * NX + x_)

    def along_x(dx, dc):
        return at(lax.rem(x + dx, NX), y, z, lax.rem(core + dc, 2))

    def along_y(dy):
        return at(x, lax.rem(y + dy, NY), z, core)

    def along_z(dz):
        return at(x, y, lax.rem(z + dz + NZ, NZ), core)

    def halo_target(dp, dz):
        band = lax.rem(pair + dp + NP, NP)
        z_ = lax.rem(lax.rem(band, 2) * ZL + zl + dz + NZ, NZ)
        return at(x, band // 2, z_, core)

    def halo_source(dp, dz):
        z_ = lax.rem(z - dz + NZ, NZ)
        band = lax.rem(y * 2 + z_ // ZL - dp + NP, NP)
        return (band * 2 + core, lax.rem(z_, ZL) * NX + x)

    mates = [(dx, dc) for dx in (0, 1, 3, 2) for dc in (1, 0) if dx or dc]
    callers = [along_x(dx, dc) for dx, dc in mates]
    callers += [along_y(d) for d in (1, 2, 3)]
    callers += [along_z(d) for d in (1, -1, 2, -2)]
    callers += [halo_source(dp, dz) for dp in (1, -1) for dz in (-1, 0, 1)]
    barrier = pltpu.get_barrier_semaphore()
    for peer in callers:
        pl.semaphore_signal(barrier, inc=1, device_id=peer, device_id_type=MESH)

    sent = []

    def keep(src, dst, sem):
        pltpu.make_async_copy(src, dst, rs.at[sem]).start()

    def send(src, dst, sem, peer):
        copy = pltpu.make_async_remote_copy(
            src_ref=src, dst_ref=dst, send_sem=ss.at[sem], recv_sem=rs.at[sem],
            device_id=peer, device_id_type=MESH)
        copy.start()
        sent.append(copy)

    def arrived(dst, sem):
        pltpu.make_async_copy(dst, dst, rs.at[sem]).wait()

    def lanes(g):
        return pl.ds(pl.multiple_of(g * PAIR, PAIR), PAIR)

    def heads_of(dx, dc):
        return lanes(lax.rem(core + dc, 2) * NX + lax.rem(x + dx, NX))

    def x_back(dx):
        return lax.rem(x + NX - dx, NX)

    edge_row = 1 + 3 * core
    inner_row = 2 + core
    both_rows = pl.ds(2 * core, 2)
    quarter = pl.ds(pl.multiple_of(y * 32, 32), 32)
    half = pl.ds(pl.multiple_of(core * 1024, 1024), 1024)
    mine = heads_of(0, 0)

    keep(flags_hbm, flags, FLAGS)
    keep(k_hbm.at[core, 0, :, mine], kb.at[edge_row, 1 + x], KE)
    keep(v_hbm.at[core, 0, :, mine], vb.at[edge_row, 1 + x], VE)
    keep(ck_hbm.at[quarter, half], zk.at[zl], CZK)
    keep(cv_hbm.at[quarter, half], zv.at[zl], CZV)
    keep(q_hbm.at[:, 0, :, mine], qb.at[both_rows, x], QQ)
    keep(k_hbm.at[1 - core, 0, :, mine], kb.at[inner_row, 1 + x], KI)
    keep(v_hbm.at[1 - core, 0, :, mine], vb.at[inner_row, 1 + x], VI)

    bias[...] = jnp.zeros(bias.shape, jnp.float32)
    arrived(flags, FLAGS)
    for t in range(2):
        kept = flags[t]
        for a in range(3):
            for b in range(3):
                cell = (slice(a, a + 1), slice(b * 128, (b + 1) * 128))
                if a == 1 and b == 1:
                    continue
                grid_row = row * 2 + t + a - 1
                grid_col = col + b - 1
                inside = ((grid_row >= 0) & (grid_row < 2 * 2 * NP)
                          & (grid_col >= 0) & (grid_col < ZL * NX))
                flag = jnp.broadcast_to(kept[:, 3 * a + b:3 * a + b + 1], (1, 128))
                usable = (flag > 0) & jnp.broadcast_to(inside, (1, 128))
                bias[(t, *cell)] = jnp.where(usable, 0.0, -jnp.inf).astype(jnp.float32)
    keep(bias, bb.at[both_rows, x], BB)

    pl.semaphore_wait(barrier, len(callers))

    for src, buf, sem, far in ((ck_hbm, zk, CZK, 2), (cv_hbm, zv, CZV, -2)):
        send(src.at[quarter, half], buf.at[zl], sem + 1, along_z(1))
        send(src.at[quarter, half], buf.at[zl], sem + 3, along_z(-1))
        send(src.at[quarter, half], buf.at[zl], sem + 2, along_z(far))
    for dx, dc in mates:
        for src, buf, sem in ((k_hbm, kb, KE), (v_hbm, vb, VE)):
            send(src.at[core, 0, :, heads_of(dx, dc)], buf.at[edge_row, 1 + x], sem + dx * 2 + dc, along_x(dx, dc))

    def forward_rows(dx):
        j = x_back(dx)
        first, last = (3 - j) // 3, j // 3
        dst_col = 1 + j + 4 * first - 4 * last
        slot = j + 4 * first + 2 * last
        for top in (0, 1):
            dc = lax.rem(core + top, 2)
            src_row, dst_row, dp = ((1, 5, -1), (4, 0, 1))[top]
            for buf, esem, sem in ((kb, KE, RK), (vb, VE, RV)):
                arrived(buf.at[src_row, 1 + j], esem + dx * 2 + dc)
                send(buf.at[src_row, 1 + j], buf.at[dst_row, dst_col], sem + top * 6 + slot,
                     halo_target(dp, last - first))

    forward_rows(0)
    for buf, sem in ((zk, CZK), (zv, CZV)):
        for dz in range(ZL):
            arrived(buf.at[lax.rem(zl + ZL - dz, ZL)], sem + dz)
    for zbuf, buf, sem in ((zk, ckb, CXK), (zv, cvb, CXV)):
        for dx in (1, 3, 2):
            send(zbuf.at[:, :, lanes(lax.rem(x + dx, NX))], buf.at[y, :, x], sem + dx, along_x(dx, 0))
        keep(zbuf.at[:, :, lanes(x)], buf.at[y, :, x], sem)
    forward_rows(1)
    forward_rows(3)
    for dx, dc in mates:
        send(q_hbm.at[:, 0, :, heads_of(dx, dc)], qb.at[both_rows, x], QQ + dx * 2 + dc, along_x(dx, dc))
    forward_rows(2)
    for dx, dc in mates:
        send(bias, bb.at[both_rows, x], BB + dx * 2 + dc, along_x(dx, dc))
        for src, buf, sem in ((k_hbm, kb, KI), (v_hbm, vb, VI)):
            send(src.at[1 - core, 0, :, heads_of(dx, dc)], buf.at[inner_row, 1 + x], sem + dx * 2 + dc, along_x(dx, dc))

    for buf, xsem, ysem in ((ckb, CXK, CYK), (cvb, CXV, CYV)):
        for dx in range(NX):
            arrived(buf.at[y, :, x_back(dx)], xsem + dx)
        for dy in (1, 3, 2):
            send(buf.at[y], buf.at[y], ysem + dy, along_y(dy))

    factor = LOG2E * HEAD_DIM ** -0.5
    contract = (((1,), (1,)), ((), ()))

    def units(i, near, coarse, start, finish):
        chains = [(j, h, slice(h * HEAD_DIM, (h + 1) * HEAD_DIM)) for j in range(4) for h in (0, 1)]
        scored = []
        for j, h, heads in chains:
            query = qb[i, j, :, heads]
            scores = []
            for a in near:
                keys = kb[i + a, j:j + 3, :, heads].reshape(3 * 128, HEAD_DIM)
                s = lax.dot_general(query, keys, contract, preferred_element_type=jnp.float32)
                scores.append(s + bb[i, j, a:a + 1, :])
            for dy in coarse:
                keys = ckb[lax.rem(y + NY - dy, NY), :, :, :, heads].reshape(512, HEAD_DIM)
                scores.append(lax.dot_general(query, keys, contract, preferred_element_type=jnp.float32))
            largest = scores[0].max(-1, keepdims=True)
            for s in scores[1:]:
                largest = jnp.maximum(largest, s.max(-1, keepdims=True))
            before = None
            if not start:
                before = mst[h, i * 4 + j]
                largest = jnp.maximum(largest, before[:, :1])
            scored.append((scores, largest, before))
        weighed = []
        for scores, largest, before in scored:
            shift = largest * factor
            total, probs = None, []
            for s in scores:
                p = jnp.exp2(s * factor - shift)
                t = p.sum(-1, keepdims=True)
                total = t if total is None else total + t
                probs.append(p.astype(jnp.bfloat16))
            weighed.append((probs, total))
        for (j, h, heads), (scores, largest, before), (probs, total) in zip(chains, scored, weighed):
            slot = i * 4 + j
            values = [vb[i + a, j:j + 3, :, heads].reshape(3 * 128, HEAD_DIM) for a in near]
            values += [cvb[lax.rem(y + NY - dy, NY), :, :, :, heads].reshape(512, HEAD_DIM) for dy in coarse]
            mixed = None
            for p, v in zip(probs, values):
                o = jnp.dot(p, v, preferred_element_type=jnp.float32)
                mixed = o if mixed is None else mixed + o
            if not start:
                scale = jnp.exp2((before - largest) * factor)
                mixed = mixed + acc[h, slot] * scale
                total = total + lst[h, slot] * scale
            if finish:
                ob[i, j, :, heads] = (mixed / total).astype(jnp.bfloat16)
            else:
                acc[h, slot] = mixed
                mst[h, slot] = jnp.broadcast_to(largest, (128, 128))
                lst[h, slot] = jnp.broadcast_to(total, (128, 128))

    def give_back(out_sem, source_row, tile_of):
        for dx in (1, 3, 2, 0):
            for dc in (1, 0):
                to_x = lax.rem(x + dx, NX)
                to_c = lax.rem(core + dc, 2)
                src = ob.at[source_row(to_c), to_x]
                dst = out_hbm.at[tile_of(to_c), 0, :, mine]
                if dx or dc:
                    send(src, dst, out_sem + dx * 2 + dc, along_x(dx, dc))
                else:
                    keep(src, dst, out_sem)

    def get_back(out_sem, tile):
        for dx in range(NX):
            for dc in (0, 1):
                g = lax.rem(core + dc, 2) * NX + x_back(dx)
                arrived(out_hbm.at[tile, 0, :, lanes(g)], out_sem + dx * 2 + dc)

    for dx in range(NX):
        for dc in (0, 1):
            rows = pl.ds(2 * lax.rem(core + dc, 2), 2)
            arrived(qb.at[rows, x_back(dx)], QQ + dx * 2 + dc)
    for buf, ysem in ((ckb, CYK), (cvb, CYV)):
        arrived(buf.at[lax.rem(y + NY - 1, NY)], ysem + 1)

    @pl.loop(0, 4)
    def _(i):
        units(i, (), (0, 1), True, False)

    for dx in range(NX):
        j = x_back(dx)
        for s in (0, 1):
            dc = lax.rem(core + s, 2)
            arrived(kb.at[2 + s, 1 + j], KI + dx * 2 + dc)
            arrived(vb.at[2 + s, 1 + j], VI + dx * 2 + dc)
    for buf, sem in ((kb, HK), (vb, HV)):
        send(buf.at[pl.ds(1, 4), 4], buf.at[pl.ds(1, 4), 0], sem, along_z(1))
        send(buf.at[pl.ds(1, 4), 1], buf.at[pl.ds(1, 4), 5], sem + 1, along_z(-1))
    for top, r in ((0, 5), (1, 0)):
        for buf, sem in ((kb, RK), (vb, RV)):
            for slot, from_col, to_col, j, dz in ((4, 5, 1, 0, 1), (5, 0, 4, 3, -1)):
                arrived(buf.at[r, from_col], sem + top * 6 + slot)
                send(buf.at[r, from_col], buf.at[r, to_col], sem + top * 6 + j, along_z(dz))

    for buf, ysem in ((ckb, CYK), (cvb, CYV)):
        for dy in (3, 2):
            arrived(buf.at[lax.rem(y + NY - dy, NY)], ysem + dy)

    @pl.loop(0, 4)
    def _(i):
        units(i, (), (2, 3), False, False)

    for dx in range(NX):
        for dc in (0, 1):
            rows = pl.ds(2 * lax.rem(core + dc, 2), 2)
            arrived(bb.at[rows, x_back(dx)], BB + dx * 2 + dc)
    for buf, sem in ((kb, HK), (vb, HV)):
        arrived(buf.at[pl.ds(1, 4), 0], sem)
        arrived(buf.at[pl.ds(1, 4), 5], sem + 1)

    @pl.loop(1, 3)
    def _(i):
        units(i, (0, 1, 2), (), False, True)

    give_back(OI, lambda c: 1 + c, lambda c: 1 - c)

    units(0, (1, 2), (), False, False)
    units(3, (0, 1), (), False, False)

    for top, r in ((1, 0), (0, 5)):
        for buf, sem in ((kb, RK), (vb, RV)):
            for j in range(4):
                arrived(buf.at[r, 1 + j], sem + top * 6 + j)

    units(0, (0,), (), False, True)
    units(3, (2,), (), False, True)

    give_back(OE, lambda c: 3 * c, lambda c: c)
    get_back(OI, 1 - core)
    get_back(OE, core)
    for copy in sent:
        copy.wait_send()


def body(queries, fine_keys, fine_values, keep_flags, coarse_keys, coarse_values):
    bf16, f32 = jnp.bfloat16, jnp.float32
    return pl.pallas_call(
        kernel,
        out_shape=jax.ShapeDtypeStruct(queries.shape, bf16),
        in_specs=[pl.BlockSpec(memory_space=pltpu.HBM)] * 6,
        out_specs=pl.BlockSpec(memory_space=pltpu.HBM),
        scratch_shapes=[
            pltpu.VMEM((4, 4, 128, PAIR), bf16),
            pltpu.VMEM((6, 6, 128, PAIR), bf16),
            pltpu.VMEM((6, 6, 128, PAIR), bf16),
            pltpu.VMEM((2, 1, 9), jnp.int32),
            pltpu.VMEM((2, 8, 384), f32),
            pltpu.VMEM((4, 4, 8, 384), f32),
            pltpu.VMEM((ZL, 32, 1024), bf16),
            pltpu.VMEM((ZL, 32, 1024), bf16),
            pltpu.VMEM((NY, ZL, NX, 32, PAIR), bf16),
            pltpu.VMEM((NY, ZL, NX, 32, PAIR), bf16),
            pltpu.VMEM((4, 4, 128, PAIR), bf16),
            pltpu.VMEM((2, 16, 128, 128), f32),
            pltpu.VMEM((2, 16, 128, 128), f32),
            pltpu.VMEM((2, 16, 128, 128), f32),
            pltpu.SemaphoreType.DMA((SEMS,)),
            pltpu.SemaphoreType.DMA((SEMS,)),
        ],
        compiler_params=pltpu.CompilerParams(
            collective_id=0, has_side_effects=True, vmem_limit_bytes=VMEM_LIMIT),
        name="window_attention",
    )(queries, fine_keys, fine_values, keep_flags, coarse_keys, coarse_values)


VMEM_LIMIT = 63 << 20


def solution(mesh):
    placed = (
        P("row", "col", None, None),
        P("row", "col", None, None),
        P("row", "col", None, None),
        P("row", "col", None),
        P("col", None),
        P("col", None),
    )
    return jax.shard_map(
        body, mesh=mesh, in_specs=placed, out_specs=P("row", "col", None, None), check_vma=False
    )
```

```python
import jax
import jax.numpy as jnp
from jax import lax
from jax.experimental import pallas as pl
from jax.experimental.pallas import tpu as pltpu
from jax.sharding import PartitionSpec as P

HEAD_DIM = 128
NX, NY, NZ = 4, 4, 8
ZL = 4
NP = 8
PAIR = 256
LOG2E = 1.4426950408889634
MESH = pl.DeviceIdType.MESH

KE, VE, KI, VI, QQ, BB = 0, 8, 16, 24, 32, 40
CZK, CZV = 48, 52
CXK, CXV = 56, 60
CYK, CYV = 64, 68
RK, RV = 72, 84
HK, HV = 96, 98
OI, OE = 100, 108
FLAGS = 116
SEMS = 117


def kernel(q_hbm, k_hbm, v_hbm, flags_hbm, ck_hbm, cv_hbm, out_hbm,
           qb, kb, vb, flags, bias, bb, zk, zv, ckb, cvb, ob, acc, mst, lst, ss, rs):
    row = lax.axis_index("row")
    col = lax.axis_index("col")
    core = lax.rem(row, 2)
    pair = row // 2
    zh = lax.rem(pair, 2)
    y = pair // 2
    x = lax.rem(col, NX)
    zl = col // NX
    z = zh * ZL + zl

    def at(x_, y_, z_, c_):
        return ((y_ * 2 + z_ // ZL) * 2 + c_, lax.rem(z_, ZL) * NX + x_)

    def along_x(dx, dc):
        return at(lax.rem(x + dx, NX), y, z, lax.rem(core + dc, 2))

    def along_y(dy):
        return at(x, lax.rem(y + dy, NY), z, core)

    def along_z(dz):
        return at(x, y, lax.rem(z + dz + NZ, NZ), core)

    def halo_target(dp, dz):
        band = lax.rem(pair + dp + NP, NP)
        z_ = lax.rem(lax.rem(band, 2) * ZL + zl + dz + NZ, NZ)
        return at(x, band // 2, z_, core)

    def halo_source(dp, dz):
        z_ = lax.rem(z - dz + NZ, NZ)
        band = lax.rem(y * 2 + z_ // ZL - dp + NP, NP)
        return (band * 2 + core, lax.rem(z_, ZL) * NX + x)

    mates = [(dx, dc) for dx in (0, 1, 3, 2) for dc in (1, 0) if dx or dc]
    callers = [along_x(dx, dc) for dx, dc in mates]
    callers += [along_y(d) for d in (1, 2, 3)]
    callers += [along_z(d) for d in (1, -1, 2, -2)]
    callers += [halo_source(dp, dz) for dp in (1, -1) for dz in (-1, 0, 1)]
    barrier = pltpu.get_barrier_semaphore()
    for peer in callers:
        pl.semaphore_signal(barrier, inc=1, device_id=peer, device_id_type=MESH)

    sent = []

    def keep(src, dst, sem):
        pltpu.make_async_copy(src, dst, rs.at[sem]).start()

    def send(src, dst, sem, peer):
        copy = pltpu.make_async_remote_copy(
            src_ref=src, dst_ref=dst, send_sem=ss.at[sem], recv_sem=rs.at[sem],
            device_id=peer, device_id_type=MESH)
        copy.start()
        sent.append(copy)

    def arrived(dst, sem):
        pltpu.make_async_copy(dst, dst, rs.at[sem]).wait()

    def lanes(g):
        return pl.ds(pl.multiple_of(g * PAIR, PAIR), PAIR)

    def heads_of(dx, dc):
        return lanes(lax.rem(core + dc, 2) * NX + lax.rem(x + dx, NX))

    def x_back(dx):
        return lax.rem(x + NX - dx, NX)

    edge_row = 1 + 3 * core
    inner_row = 2 + core
    both_rows = pl.ds(2 * core, 2)
    quarter = pl.ds(pl.multiple_of(y * 32, 32), 32)
    half = pl.ds(pl.multiple_of(core * 1024, 1024), 1024)
    mine = heads_of(0, 0)

    keep(flags_hbm, flags, FLAGS)
    keep(k_hbm.at[core, 0, :, mine], kb.at[edge_row, 1 + x], KE)
    keep(v_hbm.at[core, 0, :, mine], vb.at[edge_row, 1 + x], VE)
    keep(ck_hbm.at[quarter, half], zk.at[zl], CZK)
    keep(cv_hbm.at[quarter, half], zv.at[zl], CZV)
    keep(q_hbm.at[:, 0, :, mine], qb.at[both_rows, x], QQ)
    keep(k_hbm.at[1 - core, 0, :, mine], kb.at[inner_row, 1 + x], KI)
    keep(v_hbm.at[1 - core, 0, :, mine], vb.at[inner_row, 1 + x], VI)

    bias[...] = jnp.zeros(bias.shape, jnp.float32)
    arrived(flags, FLAGS)
    for t in range(2):
        kept = flags[t]
        for a in range(3):
            for b in range(3):
                cell = (slice(a, a + 1), slice(b * 128, (b + 1) * 128))
                if a == 1 and b == 1:
                    continue
                grid_row = row * 2 + t + a - 1
                grid_col = col + b - 1
                inside = ((grid_row >= 0) & (grid_row < 2 * 2 * NP)
                          & (grid_col >= 0) & (grid_col < ZL * NX))
                flag = jnp.broadcast_to(kept[:, 3 * a + b:3 * a + b + 1], (1, 128))
                usable = (flag > 0) & jnp.broadcast_to(inside, (1, 128))
                bias[(t, *cell)] = jnp.where(usable, 0.0, -jnp.inf).astype(jnp.float32)
    keep(bias, bb.at[both_rows, x], BB)

    pl.semaphore_wait(barrier, len(callers))

    for src, buf, sem, far in ((ck_hbm, zk, CZK, 2), (cv_hbm, zv, CZV, -2)):
        send(src.at[quarter, half], buf.at[zl], sem + 1, along_z(1))
        send(src.at[quarter, half], buf.at[zl], sem + 3, along_z(-1))
        send(src.at[quarter, half], buf.at[zl], sem + 2, along_z(far))
    for dx, dc in mates:
        for src, buf, sem in ((k_hbm, kb, KE), (v_hbm, vb, VE)):
            send(src.at[core, 0, :, heads_of(dx, dc)], buf.at[edge_row, 1 + x], sem + dx * 2 + dc, along_x(dx, dc))

    def forward_rows(dx):
        j = x_back(dx)
        first, last = (3 - j) // 3, j // 3
        dst_col = 1 + j + 4 * first - 4 * last
        slot = j + 4 * first + 2 * last
        for top in (0, 1):
            dc = lax.rem(core + top, 2)
            src_row, dst_row, dp = ((1, 5, -1), (4, 0, 1))[top]
            for buf, esem, sem in ((kb, KE, RK), (vb, VE, RV)):
                arrived(buf.at[src_row, 1 + j], esem + dx * 2 + dc)
                send(buf.at[src_row, 1 + j], buf.at[dst_row, dst_col], sem + top * 6 + slot,
                     halo_target(dp, last - first))

    forward_rows(0)
    for buf, sem in ((zk, CZK), (zv, CZV)):
        for dz in range(ZL):
            arrived(buf.at[lax.rem(zl + ZL - dz, ZL)], sem + dz)
    for zbuf, buf, sem in ((zk, ckb, CXK), (zv, cvb, CXV)):
        for dx in (1, 3, 2):
            send(zbuf.at[:, :, lanes(lax.rem(x + dx, NX))], buf.at[y, :, x], sem + dx, along_x(dx, 0))
        keep(zbuf.at[:, :, lanes(x)], buf.at[y, :, x], sem)
    forward_rows(1)
    forward_rows(3)
    for dx, dc in mates:
        for src, buf, sem in ((k_hbm, kb, KI), (v_hbm, vb, VI)):
            send(src.at[1 - core, 0, :, heads_of(dx, dc)], buf.at[inner_row, 1 + x], sem + dx * 2 + dc, along_x(dx, dc))
    forward_rows(2)
    for dx, dc in mates:
        send(q_hbm.at[:, 0, :, heads_of(dx, dc)], qb.at[both_rows, x], QQ + dx * 2 + dc, along_x(dx, dc))
        send(bias, bb.at[both_rows, x], BB + dx * 2 + dc, along_x(dx, dc))

    for buf, xsem, ysem in ((ckb, CXK, CYK), (cvb, CXV, CYV)):
        for dx in range(NX):
            arrived(buf.at[y, :, x_back(dx)], xsem + dx)
        for dy in (1, 3, 2):
            send(buf.at[y], buf.at[y], ysem + dy, along_y(dy))

    for dx in range(NX):
        j = x_back(dx)
        for s in (0, 1):
            dc = lax.rem(core + s, 2)
            arrived(kb.at[2 + s, 1 + j], KI + dx * 2 + dc)
            arrived(vb.at[2 + s, 1 + j], VI + dx * 2 + dc)
    for buf, sem in ((kb, HK), (vb, HV)):
        send(buf.at[pl.ds(1, 4), 4], buf.at[pl.ds(1, 4), 0], sem, along_z(1))
        send(buf.at[pl.ds(1, 4), 1], buf.at[pl.ds(1, 4), 5], sem + 1, along_z(-1))

    factor = LOG2E * HEAD_DIM ** -0.5
    contract = (((1,), (1,)), ((), ()))

    def units(i, near, coarse, start, finish):
        chains = [(j, h, slice(h * HEAD_DIM, (h + 1) * HEAD_DIM)) for j in range(4) for h in (0, 1)]
        scored = []
        for j, h, heads in chains:
            query = qb[i, j, :, heads]
            scores = []
            for a in near:
                keys = kb[i + a, j:j + 3, :, heads].reshape(3 * 128, HEAD_DIM)
                s = lax.dot_general(query, keys, contract, preferred_element_type=jnp.float32)
                scores.append(s + bb[i, j, pl.ds(a, 1), :])
            for dy in coarse:
                keys = ckb[lax.rem(y + NY - dy, NY), :, :, :, heads].reshape(512, HEAD_DIM)
                scores.append(lax.dot_general(query, keys, contract, preferred_element_type=jnp.float32))
            largest = scores[0].max(-1, keepdims=True)
            for s in scores[1:]:
                largest = jnp.maximum(largest, s.max(-1, keepdims=True))
            before = None
            if not start:
                before = mst[h, i * 4 + j]
                largest = jnp.maximum(largest, before[:, :1])
            scored.append((scores, largest, before))
        weighed = []
        for scores, largest, before in scored:
            shift = largest * factor
            total, probs = None, []
            for s in scores:
                p = jnp.exp2(s * factor - shift)
                t = p.sum(-1, keepdims=True)
                total = t if total is None else total + t
                probs.append(p.astype(jnp.bfloat16))
            weighed.append((probs, total))
        for (j, h, heads), (scores, largest, before), (probs, total) in zip(chains, scored, weighed):
            slot = i * 4 + j
            values = [vb[i + a, j:j + 3, :, heads].reshape(3 * 128, HEAD_DIM) for a in near]
            values += [cvb[lax.rem(y + NY - dy, NY), :, :, :, heads].reshape(512, HEAD_DIM) for dy in coarse]
            mixed = None
            for p, v in zip(probs, values):
                o = jnp.dot(p, v, preferred_element_type=jnp.float32)
                mixed = o if mixed is None else mixed + o
            if not start:
                scale = jnp.exp2((before - largest) * factor)
                mixed = mixed + acc[h, slot] * scale
                total = total + lst[h, slot] * scale
            if finish:
                ob[i, j, :, heads] = (mixed / total).astype(jnp.bfloat16)
            else:
                acc[h, slot] = mixed
                mst[h, slot] = jnp.broadcast_to(largest, (128, 128))
                lst[h, slot] = jnp.broadcast_to(total, (128, 128))

    def give_back(out_sem, source_row, tile_of):
        for dx in (1, 3, 2, 0):
            for dc in (1, 0):
                to_x = lax.rem(x + dx, NX)
                to_c = lax.rem(core + dc, 2)
                src = ob.at[source_row(to_c), to_x]
                dst = out_hbm.at[tile_of(to_c), 0, :, mine]
                if dx or dc:
                    send(src, dst, out_sem + dx * 2 + dc, along_x(dx, dc))
                else:
                    keep(src, dst, out_sem)

    def get_back(out_sem, tile):
        for dx in range(NX):
            for dc in (0, 1):
                g = lax.rem(core + dc, 2) * NX + x_back(dx)
                arrived(out_hbm.at[tile, 0, :, lanes(g)], out_sem + dx * 2 + dc)

    for dx in range(NX):
        for dc in (0, 1):
            rows = pl.ds(2 * lax.rem(core + dc, 2), 2)
            arrived(qb.at[rows, x_back(dx)], QQ + dx * 2 + dc)
    for buf, ysem in ((ckb, CYK), (cvb, CYV)):
        arrived(buf.at[lax.rem(y + NY - 1, NY)], ysem + 1)

    @pl.loop(0, 4)
    def _(i):
        units(i, (), (0, 1), True, False)

    for top, r in ((0, 5), (1, 0)):
        for buf, sem in ((kb, RK), (vb, RV)):
            for slot, from_col, to_col, j, dz in ((4, 5, 1, 0, 1), (5, 0, 4, 3, -1)):
                arrived(buf.at[r, from_col], sem + top * 6 + slot)
                send(buf.at[r, from_col], buf.at[r, to_col], sem + top * 6 + j, along_z(dz))

    for buf, ysem in ((ckb, CYK), (cvb, CYV)):
        for dy in (3, 2):
            arrived(buf.at[lax.rem(y + NY - dy, NY)], ysem + dy)

    @pl.loop(0, 4)
    def _(i):
        units(i, (), (2, 3), False, False)

    for dx in range(NX):
        for dc in (0, 1):
            rows = pl.ds(2 * lax.rem(core + dc, 2), 2)
            arrived(bb.at[rows, x_back(dx)], BB + dx * 2 + dc)
    for buf, sem in ((kb, HK), (vb, HV)):
        arrived(buf.at[pl.ds(1, 4), 0], sem)
        arrived(buf.at[pl.ds(1, 4), 5], sem + 1)

    @pl.loop(1, 3)
    def _(i):
        units(i, (0, 1, 2), (), False, True)

    give_back(OI, lambda c: 1 + c, lambda c: 1 - c)

    @pl.loop(0, 2)
    def _(u):
        units(3 * u, (1 - u, 2 - u), (), False, False)

    for top, r in ((1, 0), (0, 5)):
        for buf, sem in ((kb, RK), (vb, RV)):
            for j in range(4):
                arrived(buf.at[r, 1 + j], sem + top * 6 + j)

    def outer_back(u, dx):
        to_x = lax.rem(x + dx, NX)
        sem = OE + dx * 2 + lax.rem(core + u, 2)
        return pltpu.make_async_remote_copy(
            src_ref=ob.at[3 * u, to_x], dst_ref=out_hbm.at[u, 0, :, mine],
            send_sem=ss.at[sem], recv_sem=rs.at[sem],
            device_id=at(to_x, y, z, u), device_id_type=MESH)

    @pl.loop(0, 2)
    def _(u):
        units(3 * u, (2 * u,), (), False, True)
        for dx in (1, 3, 2):
            outer_back(u, dx).start()

    send(ob.at[3 * (1 - core), x], out_hbm.at[1 - core, 0, :, mine], OE + 1, along_x(0, 1))
    keep(ob.at[3 * core, x], out_hbm.at[core, 0, :, mine], OE)
    get_back(OI, 1 - core)
    get_back(OE, core)
    for u in (0, 1):
        for dx in (1, 2, 3):
            outer_back(u, dx).wait_send()
    for copy in sent:
        copy.wait_send()


def body(queries, fine_keys, fine_values, keep_flags, coarse_keys, coarse_values):
    bf16, f32 = jnp.bfloat16, jnp.float32
    return pl.pallas_call(
        kernel,
        out_shape=jax.ShapeDtypeStruct(queries.shape, bf16),
        in_specs=[pl.BlockSpec(memory_space=pltpu.HBM)] * 6,
        out_specs=pl.BlockSpec(memory_space=pltpu.HBM),
        scratch_shapes=[
            pltpu.VMEM((4, 4, 128, PAIR), bf16),
            pltpu.VMEM((6, 6, 128, PAIR), bf16),
            pltpu.VMEM((6, 6, 128, PAIR), bf16),
            pltpu.VMEM((2, 1, 9), jnp.int32),
            pltpu.VMEM((2, 8, 384), f32),
            pltpu.VMEM((4, 4, 8, 384), f32),
            pltpu.VMEM((ZL, 32, 1024), bf16),
            pltpu.VMEM((ZL, 32, 1024), bf16),
            pltpu.VMEM((NY, ZL, NX, 32, PAIR), bf16),
            pltpu.VMEM((NY, ZL, NX, 32, PAIR), bf16),
            pltpu.VMEM((4, 4, 128, PAIR), bf16),
            pltpu.VMEM((2, 16, 128, 128), f32),
            pltpu.VMEM((2, 16, 128, 128), f32),
            pltpu.VMEM((2, 16, 128, 128), f32),
            pltpu.SemaphoreType.DMA((SEMS,)),
            pltpu.SemaphoreType.DMA((SEMS,)),
        ],
        compiler_params=pltpu.CompilerParams(
            collective_id=0, has_side_effects=True, vmem_limit_bytes=VMEM_LIMIT),
        name="window_attention",
    )(queries, fine_keys, fine_values, keep_flags, coarse_keys, coarse_values)


VMEM_LIMIT = 63 << 20


def solution(mesh):
    placed = (
        P("row", "col", None, None),
        P("row", "col", None, None),
        P("row", "col", None, None),
        P("row", "col", None),
        P("col", None),
        P("col", None),
    )
    return jax.shard_map(
        body, mesh=mesh, in_specs=placed, out_specs=P("row", "col", None, None), check_vma=False
    )
```

```python
import jax
import jax.numpy as jnp
from jax import lax
from jax.experimental import pallas as pl
from jax.experimental.pallas import tpu as pltpu
from jax.sharding import PartitionSpec as P

HEAD_DIM = 128
NX, NY, NZ = 4, 4, 8
ZL = 4
NP = 8
PAIR = 256
LOG2E = 1.4426950408889634
MESH = pl.DeviceIdType.MESH

KE, VE, KI, VI, QQ, BB = 0, 8, 16, 24, 32, 40
CZK, CZV = 48, 52
CXK, CXV = 56, 60
CYK, CYV = 64, 68
RK, RV = 72, 84
HK, HV = 96, 98
OI, OE = 100, 108
FLAGS = 116
SEMS = 117


def kernel(q_hbm, k_hbm, v_hbm, flags_hbm, ck_hbm, cv_hbm, out_hbm,
           qb, kb, vb, flags, bias, bb, zk, zv, ckb, cvb, ob, acc, mst, lst, ss, rs):
    row = lax.axis_index("row")
    col = lax.axis_index("col")
    core = lax.rem(row, 2)
    pair = row // 2
    zh = lax.rem(pair, 2)
    y = pair // 2
    x = lax.rem(col, NX)
    zl = col // NX
    z = zh * ZL + zl

    def at(x_, y_, z_, c_):
        return ((y_ * 2 + z_ // ZL) * 2 + c_, lax.rem(z_, ZL) * NX + x_)

    def along_x(dx, dc):
        return at(lax.rem(x + dx, NX), y, z, lax.rem(core + dc, 2))

    def along_y(dy):
        return at(x, lax.rem(y + dy, NY), z, core)

    def along_z(dz):
        return at(x, y, lax.rem(z + dz + NZ, NZ), core)

    def halo_target(dp, dz):
        band = lax.rem(pair + dp + NP, NP)
        z_ = lax.rem(lax.rem(band, 2) * ZL + zl + dz + NZ, NZ)
        return at(x, band // 2, z_, core)

    def halo_source(dp, dz):
        z_ = lax.rem(z - dz + NZ, NZ)
        band = lax.rem(y * 2 + z_ // ZL - dp + NP, NP)
        return (band * 2 + core, lax.rem(z_, ZL) * NX + x)

    mates = [(dx, dc) for dx in (0, 1, 3, 2) for dc in (1, 0) if dx or dc]
    callers = [along_x(dx, dc) for dx, dc in mates]
    callers += [along_y(d) for d in (1, 2, 3)]
    callers += [along_z(d) for d in (1, -1, 2, -2)]
    callers += [halo_source(dp, dz) for dp in (1, -1) for dz in (-1, 0, 1)]
    barrier = pltpu.get_barrier_semaphore()
    for peer in callers:
        pl.semaphore_signal(barrier, inc=1, device_id=peer, device_id_type=MESH)

    sent = []

    def keep(src, dst, sem):
        pltpu.make_async_copy(src, dst, rs.at[sem]).start()

    def send(src, dst, sem, peer):
        copy = pltpu.make_async_remote_copy(
            src_ref=src, dst_ref=dst, send_sem=ss.at[sem], recv_sem=rs.at[sem],
            device_id=peer, device_id_type=MESH)
        copy.start()
        sent.append(copy)

    def arrived(dst, sem):
        pltpu.make_async_copy(dst, dst, rs.at[sem]).wait()

    def lanes(g):
        return pl.ds(pl.multiple_of(g * PAIR, PAIR), PAIR)

    def heads_of(dx, dc):
        return lanes(lax.rem(core + dc, 2) * NX + lax.rem(x + dx, NX))

    def x_back(dx):
        return lax.rem(x + NX - dx, NX)

    edge_row = 1 + 3 * core
    inner_row = 2 + core
    both_rows = pl.ds(2 * core, 2)
    quarter = pl.ds(pl.multiple_of(y * 32, 32), 32)
    half = pl.ds(pl.multiple_of(core * 1024, 1024), 1024)
    mine = heads_of(0, 0)

    keep(flags_hbm, flags, FLAGS)
    keep(k_hbm.at[core, 0, :, mine], kb.at[edge_row, 1 + x], KE)
    keep(v_hbm.at[core, 0, :, mine], vb.at[edge_row, 1 + x], VE)
    keep(ck_hbm.at[quarter, half], zk.at[zl], CZK)
    keep(cv_hbm.at[quarter, half], zv.at[zl], CZV)
    keep(q_hbm.at[:, 0, :, mine], qb.at[both_rows, x], QQ)
    keep(k_hbm.at[1 - core, 0, :, mine], kb.at[inner_row, 1 + x], KI)
    keep(v_hbm.at[1 - core, 0, :, mine], vb.at[inner_row, 1 + x], VI)

    bias[...] = jnp.zeros(bias.shape, jnp.float32)
    arrived(flags, FLAGS)
    for t in range(2):
        kept = flags[t]
        for a in range(3):
            for b in range(3):
                cell = (slice(a, a + 1), slice(b * 128, (b + 1) * 128))
                if a == 1 and b == 1:
                    continue
                grid_row = row * 2 + t + a - 1
                grid_col = col + b - 1
                inside = ((grid_row >= 0) & (grid_row < 2 * 2 * NP)
                          & (grid_col >= 0) & (grid_col < ZL * NX))
                flag = jnp.broadcast_to(kept[:, 3 * a + b:3 * a + b + 1], (1, 128))
                usable = (flag > 0) & jnp.broadcast_to(inside, (1, 128))
                bias[(t, *cell)] = jnp.where(usable, 0.0, -jnp.inf).astype(jnp.float32)
    keep(bias, bb.at[both_rows, x], BB)

    pl.semaphore_wait(barrier, len(callers))

    for src, buf, sem, far in ((ck_hbm, zk, CZK, 2), (cv_hbm, zv, CZV, -2)):
        send(src.at[quarter, half], buf.at[zl], sem + 1, along_z(1))
        send(src.at[quarter, half], buf.at[zl], sem + 3, along_z(-1))
        send(src.at[quarter, half], buf.at[zl], sem + 2, along_z(far))
    for dx, dc in mates:
        for src, buf, sem in ((k_hbm, kb, KE), (v_hbm, vb, VE)):
            send(src.at[core, 0, :, heads_of(dx, dc)], buf.at[edge_row, 1 + x], sem + dx * 2 + dc, along_x(dx, dc))

    def forward_rows(j):
        dst_col, slot, dz = {0: (5, 4, -1), 1: (2, 1, 0), 2: (3, 2, 0), 3: (0, 5, 1)}[j]
        dx = lax.rem(x + NX - j, NX)
        for top in (0, 1):
            dc = lax.rem(core + top, 2)
            src_row, dst_row, dp = ((1, 5, -1), (4, 0, 1))[top]
            for buf, esem, sem in ((kb, KE, RK), (vb, VE, RV)):
                arrived(buf.at[src_row, 1 + j], esem + dx * 2 + dc)
                send(buf.at[src_row, 1 + j], buf.at[dst_row, dst_col], sem + top * 6 + slot, halo_target(dp, dz))

    for buf, sem in ((zk, CZK), (zv, CZV)):
        for dz in range(ZL):
            arrived(buf.at[lax.rem(zl + ZL - dz, ZL)], sem + dz)
    for zbuf, buf, sem in ((zk, ckb, CXK), (zv, cvb, CXV)):
        for dx in (1, 3, 2):
            send(zbuf.at[:, :, lanes(lax.rem(x + dx, NX))], buf.at[y, :, x], sem + dx, along_x(dx, 0))
        keep(zbuf.at[:, :, lanes(x)], buf.at[y, :, x], sem)
    for dx, dc in mates:
        for src, buf, sem in ((k_hbm, kb, KI), (v_hbm, vb, VI)):
            send(src.at[1 - core, 0, :, heads_of(dx, dc)], buf.at[inner_row, 1 + x], sem + dx * 2 + dc, along_x(dx, dc))
    forward_rows(0)
    forward_rows(3)
    for dx, dc in mates:
        send(q_hbm.at[:, 0, :, heads_of(dx, dc)], qb.at[both_rows, x], QQ + dx * 2 + dc, along_x(dx, dc))
        send(bias, bb.at[both_rows, x], BB + dx * 2 + dc, along_x(dx, dc))

    for buf, xsem, ysem in ((ckb, CXK, CYK), (cvb, CXV, CYV)):
        for dx in range(NX):
            arrived(buf.at[y, :, x_back(dx)], xsem + dx)
        for dy in (1, 3, 2):
            send(buf.at[y], buf.at[y], ysem + dy, along_y(dy))

    for dx in range(NX):
        j = x_back(dx)
        for s in (0, 1):
            dc = lax.rem(core + s, 2)
            arrived(kb.at[2 + s, 1 + j], KI + dx * 2 + dc)
            arrived(vb.at[2 + s, 1 + j], VI + dx * 2 + dc)
    for buf, sem in ((kb, HK), (vb, HV)):
        send(buf.at[pl.ds(1, 4), 4], buf.at[pl.ds(1, 4), 0], sem, along_z(1))
        send(buf.at[pl.ds(1, 4), 1], buf.at[pl.ds(1, 4), 5], sem + 1, along_z(-1))
    forward_rows(1)
    forward_rows(2)

    factor = LOG2E * HEAD_DIM ** -0.5
    contract = (((1,), (1,)), ((), ()))

    def units(i, tiles, near, coarse, start, finish):
        chains = [(j, slice(h * HEAD_DIM, (h + 1) * HEAD_DIM), h) for j in tiles for h in (0, 1)]

        def scores_of(j, heads, h):
            query = qb[i, j, :, heads]
            scores = []
            for a in near:
                keys = kb[i + a, j:j + 3, :, heads].reshape(3 * 128, HEAD_DIM)
                s = lax.dot_general(query, keys, contract, preferred_element_type=jnp.float32)
                scores.append(s + bb[i, j, pl.ds(a, 1), :])
            for part in coarse:
                keys = ckb[part, :, :, :, heads].reshape(512, HEAD_DIM)
                scores.append(lax.dot_general(query, keys, contract, preferred_element_type=jnp.float32))
            largest = scores[0].max(-1, keepdims=True)
            for s in scores[1:]:
                largest = jnp.maximum(largest, s.max(-1, keepdims=True))
            before = None
            if not start:
                before = mst[h, i * 4 + j]
                largest = jnp.maximum(largest, before[:, :1])
            return scores, largest, before

        def probs_of(scores, largest, before):
            shift = largest * factor
            total, probs = None, []
            for s in scores:
                p = jnp.exp2(s * factor - shift)
                t = p.sum(-1, keepdims=True)
                total = t if total is None else total + t
                probs.append(p.astype(jnp.bfloat16))
            return probs, total

        def mix(j, heads, h, largest, before, probs, total):
            slot = i * 4 + j
            values = [vb[i + a, j:j + 3, :, heads].reshape(3 * 128, HEAD_DIM) for a in near]
            values += [cvb[part, :, :, :, heads].reshape(512, HEAD_DIM) for part in coarse]
            mixed = None
            for p, v in zip(probs, values):
                o = jnp.dot(p, v, preferred_element_type=jnp.float32)
                mixed = o if mixed is None else mixed + o
            if not start:
                scale = jnp.exp2((before - largest) * factor)
                mixed = mixed + acc[h, slot] * scale
                total = total + lst[h, slot] * scale
            if finish:
                ob[i, j, :, heads] = (mixed / total).astype(jnp.bfloat16)
            else:
                acc[h, slot] = mixed
                mst[h, slot] = jnp.broadcast_to(largest, (128, 128))
                lst[h, slot] = jnp.broadcast_to(total, (128, 128))

        if coarse:
            held = None
            for chain in chains + [None]:
                ahead = None if chain is None else (chain, scores_of(*chain))
                if held is not None:
                    (chain_, scored) = held
                    mix(*chain_, *scored[1:], *probs_of(*scored))
                held = ahead
        else:
            scored = [scores_of(*chain) for chain in chains]
            weighed = [probs_of(*sc) for sc in scored]
            for chain, sc, w in zip(chains, scored, weighed):
                mix(*chain, *sc[1:], *w)

    def give_back(out_sem, source_row, tile_of):
        for dx in (1, 3, 2, 0):
            for dc in (1, 0):
                to_x = lax.rem(x + dx, NX)
                to_c = lax.rem(core + dc, 2)
                src = ob.at[source_row(to_c), to_x]
                dst = out_hbm.at[tile_of(to_c), 0, :, mine]
                if dx or dc:
                    send(src, dst, out_sem + dx * 2 + dc, along_x(dx, dc))
                else:
                    keep(src, dst, out_sem)

    def get_back(out_sem, tile):
        for dx in range(NX):
            for dc in (0, 1):
                g = lax.rem(core + dc, 2) * NX + x_back(dx)
                arrived(out_hbm.at[tile, 0, :, lanes(g)], out_sem + dx * 2 + dc)

    for dx in range(NX):
        for dc in (0, 1):
            rows = pl.ds(2 * lax.rem(core + dc, 2), 2)
            arrived(qb.at[rows, x_back(dx)], QQ + dx * 2 + dc)
            arrived(bb.at[rows, x_back(dx)], BB + dx * 2 + dc)
    for buf, ysem in ((ckb, CYK), (cvb, CYV)):
        for dy in (1, 3, 2):
            arrived(buf.at[lax.rem(y + NY - dy, NY)], ysem + dy)
    def inner_rows(tiles):
        @pl.loop(1, 3)
        def _(i):
            units(i, tiles, (0, 1, 2), range(NY), True, True)

    def outer_rows(tiles):
        @pl.loop(0, 2)
        def _(u):
            units(3 * u, tiles, (1 - u, 2 - u), range(NY), True, False)

    inner_rows((1, 2))
    outer_rows((1, 2))

    for top, r in ((0, 5), (1, 0)):
        for buf, sem in ((kb, RK), (vb, RV)):
            for slot, from_col, to_col, j, dz in ((4, 5, 1, 0, 1), (5, 0, 4, 3, -1)):
                arrived(buf.at[r, from_col], sem + top * 6 + slot)
                send(buf.at[r, from_col], buf.at[r, to_col], sem + top * 6 + j, along_z(dz))

    for buf, sem in ((kb, HK), (vb, HV)):
        arrived(buf.at[pl.ds(1, 4), 0], sem)
        arrived(buf.at[pl.ds(1, 4), 5], sem + 1)
    inner_rows((0, 3))
    give_back(OI, lambda c: 1 + c, lambda c: 1 - c)
    outer_rows((0, 3))

    for top, r in ((1, 0), (0, 5)):
        for buf, sem in ((kb, RK), (vb, RV)):
            for j in range(4):
                arrived(buf.at[r, 1 + j], sem + top * 6 + j)

    def outer_back(u, dx):
        to_x = lax.rem(x + dx, NX)
        sem = OE + dx * 2 + lax.rem(core + u, 2)
        return pltpu.make_async_remote_copy(
            src_ref=ob.at[3 * u, to_x], dst_ref=out_hbm.at[u, 0, :, mine],
            send_sem=ss.at[sem], recv_sem=rs.at[sem],
            device_id=at(to_x, y, z, u), device_id_type=MESH)

    @pl.loop(0, 2)
    def _(u):
        units(3 * u, range(4), (2 * u,), (), False, True)
        for dx in (1, 3, 2):
            outer_back(u, dx).start()

    send(ob.at[3 * (1 - core), x], out_hbm.at[1 - core, 0, :, mine], OE + 1, along_x(0, 1))
    keep(ob.at[3 * core, x], out_hbm.at[core, 0, :, mine], OE)
    get_back(OI, 1 - core)
    get_back(OE, core)
    for u in (0, 1):
        for dx in (1, 2, 3):
            outer_back(u, dx).wait_send()
    for copy in sent:
        copy.wait_send()


def body(queries, fine_keys, fine_values, keep_flags, coarse_keys, coarse_values):
    bf16, f32 = jnp.bfloat16, jnp.float32
    return pl.pallas_call(
        kernel,
        out_shape=jax.ShapeDtypeStruct(queries.shape, bf16),
        in_specs=[pl.BlockSpec(memory_space=pltpu.HBM)] * 6,
        out_specs=pl.BlockSpec(memory_space=pltpu.HBM),
        scratch_shapes=[
            pltpu.VMEM((4, 4, 128, PAIR), bf16),
            pltpu.VMEM((6, 6, 128, PAIR), bf16),
            pltpu.VMEM((6, 6, 128, PAIR), bf16),
            pltpu.VMEM((2, 1, 9), jnp.int32),
            pltpu.VMEM((2, 8, 384), f32),
            pltpu.VMEM((4, 4, 8, 384), f32),
            pltpu.VMEM((ZL, 32, 1024), bf16),
            pltpu.VMEM((ZL, 32, 1024), bf16),
            pltpu.VMEM((NY, ZL, NX, 32, PAIR), bf16),
            pltpu.VMEM((NY, ZL, NX, 32, PAIR), bf16),
            pltpu.VMEM((4, 4, 128, PAIR), bf16),
            pltpu.VMEM((2, 16, 128, 128), f32),
            pltpu.VMEM((2, 16, 128, 128), f32),
            pltpu.VMEM((2, 16, 128, 128), f32),
            pltpu.SemaphoreType.DMA((SEMS,)),
            pltpu.SemaphoreType.DMA((SEMS,)),
        ],
        compiler_params=pltpu.CompilerParams(
            collective_id=0, has_side_effects=True, vmem_limit_bytes=VMEM_LIMIT),
        name="window_attention",
    )(queries, fine_keys, fine_values, keep_flags, coarse_keys, coarse_values)


VMEM_LIMIT = 63 << 20


def solution(mesh):
    placed = (
        P("row", "col", None, None),
        P("row", "col", None, None),
        P("row", "col", None, None),
        P("row", "col", None),
        P("col", None),
        P("col", None),
    )
    return jax.shard_map(
        body, mesh=mesh, in_specs=placed, out_specs=P("row", "col", None, None), check_vma=False
    )
```

```python
import jax
import jax.numpy as jnp
from jax import lax
from jax.experimental import pallas as pl
from jax.experimental.pallas import tpu as pltpu
from jax.sharding import PartitionSpec as P

HEAD_DIM = 128
NX, NY, NZ = 4, 4, 8
ZL = 4
NP = 8
PAIR = 256
LOG2E = 1.4426950408889634
MESH = pl.DeviceIdType.MESH

KE, VE, KI, VI, QQ, BB = 0, 8, 16, 24, 32, 40
CZK, CZV = 48, 52
CXK, CXV = 56, 60
CYK, CYV = 64, 68
RK, RV = 72, 84
HK, HV = 96, 98
OI, OE = 100, 108
FLAGS = 116
SEMS = 117


def kernel(q_hbm, k_hbm, v_hbm, flags_hbm, ck_hbm, cv_hbm, out_hbm,
           qb, kb, vb, flags, bias, bb, zk, zv, ckb, cvb, ob, acc, mst, lst, ss, rs):
    row = lax.axis_index("row")
    col = lax.axis_index("col")
    core = lax.rem(row, 2)
    pair = row // 2
    zh = lax.rem(pair, 2)
    y = pair // 2
    x = lax.rem(col, NX)
    zl = col // NX
    z = zh * ZL + zl

    def at(x_, y_, z_, c_):
        return ((y_ * 2 + z_ // ZL) * 2 + c_, lax.rem(z_, ZL) * NX + x_)

    def along_x(dx, dc):
        return at(lax.rem(x + dx, NX), y, z, lax.rem(core + dc, 2))

    def along_y(dy):
        return at(x, lax.rem(y + dy, NY), z, core)

    def along_z(dz):
        return at(x, y, lax.rem(z + dz + NZ, NZ), core)

    def halo_target(dp, dz):
        band = lax.rem(pair + dp + NP, NP)
        z_ = lax.rem(lax.rem(band, 2) * ZL + zl + dz + NZ, NZ)
        return at(x, band // 2, z_, core)

    def halo_source(dp, dz):
        z_ = lax.rem(z - dz + NZ, NZ)
        band = lax.rem(y * 2 + z_ // ZL - dp + NP, NP)
        return (band * 2 + core, lax.rem(z_, ZL) * NX + x)

    mates = [(dx, dc) for dx in (0, 1, 3, 2) for dc in (1, 0) if dx or dc]
    callers = [along_x(dx, dc) for dx, dc in mates]
    callers += [along_y(d) for d in (1, 2, 3)]
    callers += [along_z(d) for d in (1, -1, 2, -2)]
    callers += [halo_source(dp, dz) for dp in (1, -1) for dz in (-1, 0, 1)]
    barrier = pltpu.get_barrier_semaphore()
    for peer in callers:
        pl.semaphore_signal(barrier, inc=1, device_id=peer, device_id_type=MESH)

    sent = []

    def keep(src, dst, sem):
        pltpu.make_async_copy(src, dst, rs.at[sem]).start()

    def send(src, dst, sem, peer):
        copy = pltpu.make_async_remote_copy(
            src_ref=src, dst_ref=dst, send_sem=ss.at[sem], recv_sem=rs.at[sem],
            device_id=peer, device_id_type=MESH)
        copy.start()
        sent.append(copy)

    def arrived(dst, sem):
        pltpu.make_async_copy(dst, dst, rs.at[sem]).wait()

    def lanes(g):
        return pl.ds(pl.multiple_of(g * PAIR, PAIR), PAIR)

    def heads_of(dx, dc):
        return lanes(lax.rem(core + dc, 2) * NX + lax.rem(x + dx, NX))

    def x_back(dx):
        return lax.rem(x + NX - dx, NX)

    edge_row = 1 + 3 * core
    inner_row = 2 + core
    both_rows = pl.ds(2 * core, 2)
    quarter = pl.ds(pl.multiple_of(y * 32, 32), 32)
    half = pl.ds(pl.multiple_of(core * 1024, 1024), 1024)
    mine = heads_of(0, 0)

    keep(flags_hbm, flags, FLAGS)
    keep(k_hbm.at[core, 0, :, mine], kb.at[edge_row, 1 + x], KE)
    keep(v_hbm.at[core, 0, :, mine], vb.at[edge_row, 1 + x], VE)
    keep(ck_hbm.at[quarter, half], zk.at[zl], CZK)
    keep(cv_hbm.at[quarter, half], zv.at[zl], CZV)
    keep(q_hbm.at[:, 0, :, mine], qb.at[both_rows, x], QQ)
    keep(k_hbm.at[1 - core, 0, :, mine], kb.at[inner_row, 1 + x], KI)
    keep(v_hbm.at[1 - core, 0, :, mine], vb.at[inner_row, 1 + x], VI)

    bias[...] = jnp.zeros(bias.shape, jnp.float32)
    arrived(flags, FLAGS)
    for t in range(2):
        kept = flags[t]
        for a in range(3):
            for b in range(3):
                cell = (slice(a, a + 1), slice(b * 128, (b + 1) * 128))
                if a == 1 and b == 1:
                    continue
                grid_row = row * 2 + t + a - 1
                grid_col = col + b - 1
                inside = ((grid_row >= 0) & (grid_row < 2 * 2 * NP)
                          & (grid_col >= 0) & (grid_col < ZL * NX))
                flag = jnp.broadcast_to(kept[:, 3 * a + b:3 * a + b + 1], (1, 128))
                usable = (flag > 0) & jnp.broadcast_to(inside, (1, 128))
                bias[(t, *cell)] = jnp.where(usable, 0.0, -jnp.inf).astype(jnp.float32)
    keep(bias, bb.at[both_rows, x], BB)

    pl.semaphore_wait(barrier, len(callers))

    for src, buf, sem, far in ((ck_hbm, zk, CZK, 2), (cv_hbm, zv, CZV, -2)):
        send(src.at[quarter, half], buf.at[zl], sem + 1, along_z(1))
        send(src.at[quarter, half], buf.at[zl], sem + 3, along_z(-1))
        send(src.at[quarter, half], buf.at[zl], sem + 2, along_z(far))
    for dx, dc in mates:
        for src, buf, sem in ((k_hbm, kb, KE), (v_hbm, vb, VE)):
            send(src.at[core, 0, :, heads_of(dx, dc)], buf.at[edge_row, 1 + x], sem + dx * 2 + dc, along_x(dx, dc))

    def forward_rows(j):
        dst_col, slot, dz = {0: (5, 4, -1), 1: (2, 1, 0), 2: (3, 2, 0), 3: (0, 5, 1)}[j]
        dx = lax.rem(x + NX - j, NX)
        for top in (0, 1):
            dc = lax.rem(core + top, 2)
            src_row, dst_row, dp = ((1, 5, -1), (4, 0, 1))[top]
            for buf, esem, sem in ((kb, KE, RK), (vb, VE, RV)):
                arrived(buf.at[src_row, 1 + j], esem + dx * 2 + dc)
                send(buf.at[src_row, 1 + j], buf.at[dst_row, dst_col], sem + top * 6 + slot, halo_target(dp, dz))

    for buf, sem in ((zk, CZK), (zv, CZV)):
        for dz in range(ZL):
            arrived(buf.at[lax.rem(zl + ZL - dz, ZL)], sem + dz)
    for zbuf, buf, sem in ((zk, ckb, CXK), (zv, cvb, CXV)):
        for dx in (1, 3, 2):
            send(zbuf.at[:, :, lanes(lax.rem(x + dx, NX))], buf.at[y, :, x], sem + dx, along_x(dx, 0))
        keep(zbuf.at[:, :, lanes(x)], buf.at[y, :, x], sem)
    for dx, dc in mates:
        for src, buf, sem in ((k_hbm, kb, KI), (v_hbm, vb, VI)):
            send(src.at[1 - core, 0, :, heads_of(dx, dc)], buf.at[inner_row, 1 + x], sem + dx * 2 + dc, along_x(dx, dc))
    forward_rows(0)
    forward_rows(3)
    for dx, dc in mates:
        send(q_hbm.at[:, 0, :, heads_of(dx, dc)], qb.at[both_rows, x], QQ + dx * 2 + dc, along_x(dx, dc))
        send(bias, bb.at[both_rows, x], BB + dx * 2 + dc, along_x(dx, dc))

    for buf, xsem, ysem in ((ckb, CXK, CYK), (cvb, CXV, CYV)):
        for dx in range(NX):
            arrived(buf.at[y, :, x_back(dx)], xsem + dx)
        for dy in (1, 3, 2):
            send(buf.at[y], buf.at[y], ysem + dy, along_y(dy))

    def inner_tiles(j):
        dx = lax.rem(x + NX - j, NX)
        for s in (0, 1):
            dc = lax.rem(core + s, 2)
            arrived(kb.at[2 + s, 1 + j], KI + dx * 2 + dc)
            arrived(vb.at[2 + s, 1 + j], VI + dx * 2 + dc)

    inner_tiles(0)
    inner_tiles(3)
    for buf, sem in ((kb, HK), (vb, HV)):
        send(buf.at[pl.ds(1, 4), 4], buf.at[pl.ds(1, 4), 0], sem, along_z(1))
        send(buf.at[pl.ds(1, 4), 1], buf.at[pl.ds(1, 4), 5], sem + 1, along_z(-1))
    forward_rows(1)
    forward_rows(2)
    inner_tiles(1)
    inner_tiles(2)

    factor = LOG2E * HEAD_DIM ** -0.5
    contract = (((1,), (1,)), ((), ()))

    def units(i, tiles, near, coarse, start, finish):
        chains = [(j, slice(h * HEAD_DIM, (h + 1) * HEAD_DIM), h) for j in tiles for h in (0, 1)]

        def scores_of(j, heads, h):
            query = qb[i, j, :, heads]
            scores = []
            for a in near:
                keys = kb[i + a, j:j + 3, :, heads].reshape(3 * 128, HEAD_DIM)
                s = lax.dot_general(query, keys, contract, preferred_element_type=jnp.float32)
                scores.append(s + bb[i, j, pl.ds(a, 1), :])
            for part in coarse:
                keys = ckb[part, :, :, :, heads].reshape(512, HEAD_DIM)
                scores.append(lax.dot_general(query, keys, contract, preferred_element_type=jnp.float32))
            largest = scores[0].max(-1, keepdims=True)
            for s in scores[1:]:
                largest = jnp.maximum(largest, s.max(-1, keepdims=True))
            before = None
            if not start:
                before = mst[h, i * 4 + j]
                largest = jnp.maximum(largest, before[:, :1])
            return scores, largest, before

        def probs_of(scores, largest, before):
            shift = largest * factor
            total, probs = None, []
            for s in scores:
                p = jnp.exp2(s * factor - shift)
                t = p.sum(-1, keepdims=True)
                total = t if total is None else total + t
                probs.append(p.astype(jnp.bfloat16))
            return probs, total

        def mix(j, heads, h, largest, before, probs, total):
            slot = i * 4 + j
            values = [vb[i + a, j:j + 3, :, heads].reshape(3 * 128, HEAD_DIM) for a in near]
            values += [cvb[part, :, :, :, heads].reshape(512, HEAD_DIM) for part in coarse]
            mixed = None
            for p, v in zip(probs, values):
                o = jnp.dot(p, v, preferred_element_type=jnp.float32)
                mixed = o if mixed is None else mixed + o
            if not start:
                scale = jnp.exp2((before - largest) * factor)
                mixed = mixed + acc[h, slot] * scale
                total = total + lst[h, slot] * scale
            if finish:
                ob[i, j, :, heads] = (mixed / total).astype(jnp.bfloat16)
            else:
                acc[h, slot] = mixed
                mst[h, slot] = jnp.broadcast_to(largest, (128, 128))
                lst[h, slot] = jnp.broadcast_to(total, (128, 128))

        if coarse:
            held = None
            for chain in chains + [None]:
                ahead = None if chain is None else (chain, scores_of(*chain))
                if held is not None:
                    (chain_, scored) = held
                    mix(*chain_, *scored[1:], *probs_of(*scored))
                held = ahead
        else:
            scored = [scores_of(*chain) for chain in chains]
            weighed = [probs_of(*sc) for sc in scored]
            for chain, sc, w in zip(chains, scored, weighed):
                mix(*chain, *sc[1:], *w)

    def give_back(out_sem, source_row, tile_of):
        for dx in (1, 3, 2, 0):
            for dc in (1, 0):
                to_x = lax.rem(x + dx, NX)
                to_c = lax.rem(core + dc, 2)
                src = ob.at[source_row(to_c), to_x]
                dst = out_hbm.at[tile_of(to_c), 0, :, mine]
                if dx or dc:
                    send(src, dst, out_sem + dx * 2 + dc, along_x(dx, dc))
                else:
                    keep(src, dst, out_sem)

    def get_back(out_sem, tile):
        for dx in range(NX):
            for dc in (0, 1):
                g = lax.rem(core + dc, 2) * NX + x_back(dx)
                arrived(out_hbm.at[tile, 0, :, lanes(g)], out_sem + dx * 2 + dc)

    for dx in range(NX):
        for dc in (0, 1):
            rows = pl.ds(2 * lax.rem(core + dc, 2), 2)
            arrived(qb.at[rows, x_back(dx)], QQ + dx * 2 + dc)
            arrived(bb.at[rows, x_back(dx)], BB + dx * 2 + dc)
    for buf, ysem in ((ckb, CYK), (cvb, CYV)):
        for dy in (1, 3, 2):
            arrived(buf.at[lax.rem(y + NY - dy, NY)], ysem + dy)
    def inner_rows(tiles):
        @pl.loop(1, 3)
        def _(i):
            units(i, tiles, (0, 1, 2), range(NY), True, True)

    def outer_rows(tiles):
        @pl.loop(0, 2)
        def _(u):
            units(3 * u, tiles, (1 - u, 2 - u), range(NY), True, False)

    inner_rows((1, 2))
    outer_rows((1, 2))

    for top, r in ((0, 5), (1, 0)):
        for buf, sem in ((kb, RK), (vb, RV)):
            for slot, from_col, to_col, j, dz in ((4, 5, 1, 0, 1), (5, 0, 4, 3, -1)):
                arrived(buf.at[r, from_col], sem + top * 6 + slot)
                send(buf.at[r, from_col], buf.at[r, to_col], sem + top * 6 + j, along_z(dz))

    for buf, sem in ((kb, HK), (vb, HV)):
        arrived(buf.at[pl.ds(1, 4), 0], sem)
        arrived(buf.at[pl.ds(1, 4), 5], sem + 1)
    inner_rows((0, 3))
    give_back(OI, lambda c: 1 + c, lambda c: 1 - c)
    outer_rows((0, 3))


    def outer_back(u, dx):
        to_x = lax.rem(x + dx, NX)
        sem = OE + dx * 2 + lax.rem(core + u, 2)
        return pltpu.make_async_remote_copy(
            src_ref=ob.at[3 * u, to_x], dst_ref=out_hbm.at[u, 0, :, mine],
            send_sem=ss.at[sem], recv_sem=rs.at[sem],
            device_id=at(to_x, y, z, u), device_id_type=MESH)

    @pl.loop(0, 2)
    def _(u):
        for buf, sem in ((kb, RK), (vb, RV)):
            for j in range(4):
                arrived(buf.at[5 * u, 1 + j], sem + (1 - u) * 6 + j)
        units(3 * u, range(4), (2 * u,), (), False, True)
        for dx in (1, 3, 2):
            outer_back(u, dx).start()

    send(ob.at[3 * (1 - core), x], out_hbm.at[1 - core, 0, :, mine], OE + 1, along_x(0, 1))
    keep(ob.at[3 * core, x], out_hbm.at[core, 0, :, mine], OE)
    get_back(OI, 1 - core)
    get_back(OE, core)
    for u in (0, 1):
        for dx in (1, 2, 3):
            outer_back(u, dx).wait_send()
    for copy in sent:
        copy.wait_send()


def body(queries, fine_keys, fine_values, keep_flags, coarse_keys, coarse_values):
    bf16, f32 = jnp.bfloat16, jnp.float32
    return pl.pallas_call(
        kernel,
        out_shape=jax.ShapeDtypeStruct(queries.shape, bf16),
        in_specs=[pl.BlockSpec(memory_space=pltpu.HBM)] * 6,
        out_specs=pl.BlockSpec(memory_space=pltpu.HBM),
        scratch_shapes=[
            pltpu.VMEM((4, 4, 128, PAIR), bf16),
            pltpu.VMEM((6, 6, 128, PAIR), bf16),
            pltpu.VMEM((6, 6, 128, PAIR), bf16),
            pltpu.VMEM((2, 1, 9), jnp.int32),
            pltpu.VMEM((2, 8, 384), f32),
            pltpu.VMEM((4, 4, 8, 384), f32),
            pltpu.VMEM((ZL, 32, 1024), bf16),
            pltpu.VMEM((ZL, 32, 1024), bf16),
            pltpu.VMEM((NY, ZL, NX, 32, PAIR), bf16),
            pltpu.VMEM((NY, ZL, NX, 32, PAIR), bf16),
            pltpu.VMEM((4, 4, 128, PAIR), bf16),
            pltpu.VMEM((2, 16, 128, 128), f32),
            pltpu.VMEM((2, 16, 128, 128), f32),
            pltpu.VMEM((2, 16, 128, 128), f32),
            pltpu.SemaphoreType.DMA((SEMS,)),
            pltpu.SemaphoreType.DMA((SEMS,)),
        ],
        compiler_params=pltpu.CompilerParams(
            collective_id=0, has_side_effects=True, vmem_limit_bytes=VMEM_LIMIT),
        name="window_attention",
    )(queries, fine_keys, fine_values, keep_flags, coarse_keys, coarse_values)


VMEM_LIMIT = 63 << 20


def solution(mesh):
    placed = (
        P("row", "col", None, None),
        P("row", "col", None, None),
        P("row", "col", None, None),
        P("row", "col", None),
        P("col", None),
        P("col", None),
    )
    return jax.shard_map(
        body, mesh=mesh, in_specs=placed, out_specs=P("row", "col", None, None), check_vma=False
    )
```
